32 devices in a mesh: mem: 2 (over x), lat: 4 (over z), lon: 4 (over y, core).
Axes of the slice: x: 2, y: 2, z: 4, core: 2. Of those that a mesh axis runs over, the one named last changes fastest.
Arguments:
- control: bfloat16 [8, 256, 128, 128], P('mem', 'lat', 'lon'), may hold values from -21 to 21
- ensemble: bfloat16 [8, 256, 128, 128], P('mem', 'lat', 'lon'), may hold values from -3 to 3
- precision: float32 [256, 128, 128], P('lat', 'lon'), may hold values from 0.5 to 8
- lat_taps: float32 [9], replicated, may hold values from 0.05 to 0.3
- lon_taps: float32 [9], replicated, may hold values from 0.05 to 0.3
- vertical: bfloat16 [128, 128], replicated, may hold values from -0.5 to 0.5
Outputs:
- hessian: float32 [8, 256, 128, 128], P('mem', 'lat', 'lon')
- curvature: float32 [], replicated
The draws below stay inside these ranges and needn't reach their ends.
All inputs are finite; a program needn't handle non-finite values.
Results may differ from the reference program's by a relative error of at most 0.0038.
Values may be sent and summed in bfloat16 or wider, within the bound.
A program may use at most 64 MiB of HBM per device.

```python
import math
import jax
import jax.numpy as jnp
from jax import lax

LV = 128
TAPS = 9
MEMBERS = 8
NLAT = 256
NLON = 128


def draw_control(key, part):
    first_key = jax.random.fold_in(jax.random.fold_in(key, 11), 0)
    shape = (MEMBERS, NLAT, NLON, LV)
    member_pos = jnp.arange(MEMBERS, dtype=jnp.float32) / max(MEMBERS - 1, 1)
    lat_pos = jnp.arange(NLAT, dtype=jnp.float32) / max(NLAT - 1, 1)
    lon_pos = jnp.arange(NLON, dtype=jnp.float32) / max(NLON - 1, 1)
    exponent = member_pos[:, None, None, None] + lat_pos[None, :, None, None] + lon_pos[None, None, :, None]
    scaling = jnp.exp(0.5 * jnp.log(3.0) * exponent)
    base = jax.random.normal(first_key, shape, jnp.float32)
    base = jnp.clip(base, -4.0, 4.0)
    return (base * scaling).astype(jnp.bfloat16)


def block_scale(stream_key, dims, cuts, low, largest):
    level = 1.0
    for axis_at, shards_of in cuts:
        heights = jax.random.uniform(jax.random.fold_in(jax.random.fold_in(stream_key, 6), axis_at), (shards_of,), jnp.float32, low / len(cuts), largest / len(cuts))
        level = level * jnp.repeat(jnp.exp(heights), dims[axis_at] // shards_of).reshape((-1,) + (1,) * (len(dims) - 1 - axis_at))
    return level


def centred(key, dims, deviation, reach, shards=(), held_as=jnp.bfloat16):
    values = deviation * jax.random.normal(key, dims, jnp.float32)
    if shards:
        values = values * block_scale(key, dims, shards, -0.22, 0.18)
    return jnp.clip(values, -reach, reach).astype(held_as)


def setup_inputs(seed: int = 0) -> dict:
    streams_of = jax.random.split(jax.random.key(seed), 7)
    control = draw_control(jax.random.fold_in(streams_of[6], 71), 0)
    ensemble = centred(streams_of[1], (MEMBERS, NLAT, NLON, LV), 0.5, 3.0, ((0, 2), (1, 4), (2, 4)))
    precision = jnp.clip(jnp.exp(math.log(8.0) - 2.7725887 * jax.random.uniform(streams_of[2], (NLAT, NLON, LV), jnp.float32) ** block_scale(streams_of[2], (NLAT, NLON, LV), ((0, 4), (1, 4)), -0.2, 0.2)), 0.5, 8.0)
    lat_taps = jnp.clip(jnp.exp(jax.random.uniform(streams_of[3], (TAPS,), jnp.float32, math.log(0.05), math.log(0.3))), 0.05, 0.3)
    lon_taps = jnp.clip(jnp.exp(jax.random.uniform(streams_of[4], (TAPS,), jnp.float32, math.log(0.05), math.log(0.3))), 0.05, 0.3)
    vertical = centred(streams_of[5], (LV, LV), LV ** -0.5, 0.5)
    return dict(control=control, ensemble=ensemble, precision=precision, lat_taps=lat_taps, lon_taps=lon_taps, vertical=vertical)


def smooth_member(values, first_taps, second_taps):
    padded = jnp.pad(values, ((4, 4), (0, 0), (0, 0)))
    padded = jnp.concatenate([padded[:, -4:], padded, padded[:, :4]], axis=1)
    across = first_taps[0] * padded[0:NLAT]
    for offset in range(1, TAPS):
        across = across + first_taps[offset] * padded[offset:offset + NLAT]
    result = second_taps[0] * across[:, 0:NLON]
    for offset in range(1, TAPS):
        result = result + second_taps[offset] * across[:, offset:offset + NLON]
    return result


def reference(control, ensemble, precision, lat_taps, lon_taps, vertical):
    def forward(running, inputs):
        member, spread = inputs
        smoothed = smooth_member(member, lat_taps, lon_taps).astype(jnp.bfloat16)
        leveled = jnp.dot(smoothed.reshape(-1, LV), vertical, preferred_element_type=jnp.float32).reshape(smoothed.shape)
        return running + spread * leveled, None

    increment, unused = lax.scan(forward, jnp.zeros((NLAT, NLON, LV), jnp.float32), (control, ensemble))
    weighted = precision * increment

    def adjoint(inputs):
        member, spread = inputs
        member_part = (spread * weighted).astype(jnp.bfloat16)
        adjoint_lev = jnp.dot(member_part.reshape(-1, LV), vertical.T, preferred_element_type=jnp.float32)
        adjoint_lev = adjoint_lev.reshape(member_part.shape).astype(jnp.bfloat16)
        back = smooth_member(adjoint_lev, lat_taps[::-1], lon_taps[::-1])
        hessian = member + back
        return hessian, jnp.sum(member * hessian)

    hessian, terms = lax.map(adjoint, (control, ensemble))
    curvature = jnp.sum(terms) / (MEMBERS * NLAT * NLON * LV)
    return hessian, curvature
```

```python
import functools
import itertools
import math

import jax
import jax.numpy as jnp
from jax import lax
from jax.experimental import pallas as pl
from jax.experimental.pallas import tpu as pltpu
from jax.sharding import PartitionSpec as P

F32 = jnp.float32
BF16 = jnp.bfloat16
HALF = 4


def iota(shape, dim):
    return lax.broadcasted_iota(jnp.int32, shape, dim)


def filter_matrix(lat_taps, lon_taps, cols, reverse):
    taps = lat_taps.shape[0]
    shape = (HALF * cols, 3 * HALF * cols + 6 * HALF * HALF)
    out, src = iota(shape, 0), iota(shape, 1)
    main = 3 * HALF * cols
    side = 3 * HALF * HALF
    inside = src < main
    left = src < main + side
    packed = jnp.where(left, src - main, src - main - side)
    row = jnp.where(inside, src // cols, packed // HALF)
    col = jnp.where(
        inside, src % cols, packed % HALF + jnp.where(left, -HALF, cols)
    )
    down = row - out // cols
    across = col - out % cols + HALF
    first = jnp.zeros(shape, F32)
    second = jnp.zeros(shape, F32)
    for tap in range(taps):
        at = taps - 1 - tap if reverse else tap
        first = jnp.where(down == tap, lat_taps[at], first)
        second = jnp.where(across == tap, lon_taps[at], second)
    full = first * second
    high = full.astype(BF16)
    low = (full - high.astype(F32)).astype(BF16)
    return jnp.concatenate([high, low], axis=0)


def border_matrix(lat_taps, lon_taps, cols):
    taps = lat_taps.shape[0]
    tile = 2 * HALF
    side = 3 * HALF * HALF
    shape = (2 * tile * HALF, 2 * side)
    out, src = iota(shape, 0), iota(shape, 1)
    place = out % (2 * tile)
    left = src < side
    packed = jnp.where(left, src, src - side)
    down = packed // HALF - out // (2 * tile)
    col = packed % HALF + jnp.where(left, -HALF, cols)
    across = col - (place + jnp.where(place < tile, 0, cols - 2 * tile)) + HALF
    first = jnp.zeros(shape, F32)
    second = jnp.zeros(shape, F32)
    for tap in range(taps):
        first = jnp.where(down == tap, lat_taps[tap], first)
        second = jnp.where(across == tap, lon_taps[tap], second)
    full = first * second
    high = full.astype(BF16)
    low = (full - high.astype(F32)).astype(BF16)
    return jnp.concatenate([high, low], axis=0)


def dot(a, b):
    return jnp.dot(a, b, preferred_element_type=F32)


def kernel(
    axes, sizes, entries, chunks, lat_taps, lon_taps, control, ensemble, precision, vertical, hess, curv,
    ext, ext2, ens, prec, own_in, own_rim, wgt, inner_out, rim_out, inner_in, rim_in, keep, halo, halo2, stage, stage2,
    filt, filt2, border, vert, vert2, vert2t, sums, parts, taps1, taps2,
    local_sem, send_sem, recv_sem, side_send, side_recv, inc_send, inc_recv, part_send, part_recv,
):
    members, rows, cols, levels = control.shape
    groups = rows // HALF
    per = groups // chunks
    cells = HALF * cols
    width = 2 if members % 2 == 0 else 1
    me = {a: lax.axis_index(a) for a in axes}
    n = dict(zip(axes, sizes))

    def device(**at):
        return tuple(at.get(a, me[a]) for a in axes)

    def place(to):
        index = 0
        for size, at in zip(sizes, to):
            index = index * size + at
        return index

    lat, lon = me["lat"], me["lon"]
    left = lax.rem(lon + n["lon"] - 1, n["lon"])
    right = lax.rem(lon + 1, n["lon"])
    has_up = lat > 0
    has_down = lat < n["lat"] - 1
    steps = [s for s in itertools.product(*(range(size) for size in sizes)) if any(s)]

    def ahead(step):
        return tuple(lax.rem(me[a] + d, n[a]) if d else me[a] for a, d in zip(axes, step))

    loads = [
        pltpu.make_async_copy(control, ext.at[:, pl.ds(HALF, rows)], local_sem.at[0]),
        pltpu.make_async_copy(vertical, vert, local_sem.at[1]),
        pltpu.make_async_copy(ensemble, ens, local_sem.at[2]),
        pltpu.make_async_copy(precision, prec, local_sem.at[3]),
        pltpu.make_async_copy(lat_taps, taps1, local_sem.at[4]),
        pltpu.make_async_copy(lon_taps, taps2, local_sem.at[5]),
    ]
    for at in (4, 5, 0, 1, 2, 3):
        loads[at].start()

    barrier = pltpu.get_barrier_semaphore()
    for step in steps:
        pl.semaphore_signal(barrier, inc=1, device_id=ahead(step), device_id_type=pl.DeviceIdType.MESH)

    def remote(src, dst, send, recv, to):
        return pltpu.make_async_remote_copy(
            src_ref=src, dst_ref=dst, send_sem=send, recv_sem=recv,
            device_id=to, device_id_type=pl.DeviceIdType.MESH,
        )

    def row_copies(phase, up_src, down_src, dst):
        up = remote(
            up_src, dst.at[:, pl.ds(rows + HALF, HALF)],
            send_sem.at[phase, 0], recv_sem.at[phase, 0], device(lat=lat - 1),
        )
        down = remote(
            down_src, dst.at[:, pl.ds(0, HALF)],
            send_sem.at[phase, 1], recv_sem.at[phase, 1], device(lat=lat + 1),
        )
        return [up], [down]

    def corner_copies(phase, src, dst):
        up, down = [], []
        for side, to in ((0, left), (1, right)):
            there = dst.at[1 - side]
            mine = src.at[side]
            up.append(remote(
                mine.at[:, 0], there.at[:, groups + 1],
                send_sem.at[phase, 2 + side], recv_sem.at[phase, 2 + side], device(lat=lat - 1, lon=to),
            ))
            down.append(remote(
                mine.at[:, groups - 1], there.at[:, 0],
                send_sem.at[phase, 4 + side], recv_sem.at[phase, 4 + side], device(lat=lat + 1, lon=to),
            ))
        return up, down

    def side_copies(phase, src, dst, chunk):
        return [
            remote(
                src.at[side, :, pl.ds(chunk * per, per)], dst.at[1 - side, :, pl.ds(chunk * per + 1, per)],
                side_send.at[phase, side, chunk], side_recv.at[phase, side, chunk], device(lon=to),
            )
            for side, to in ((0, left), (1, right))
        ]

    def inc_copies(chunk, part):
        at = pl.ds(chunk * per, per)
        out, into = ((inner_out, inner_in), (rim_out, rim_in))[part]
        return [
            remote(
                out.at[at], into.at[step - 1, at],
                inc_send.at[part, step - 1, chunk], inc_recv.at[part, step - 1, chunk],
                device(mem=lax.rem(me["mem"] + step, n["mem"])),
            )
            for step in range(1, n["mem"])
        ]

    def each(has, copies, act):
        @pl.when(has)
        def _():
            for copy in copies:
                getattr(copy, act)()

    @pl.when(jnp.logical_not(has_up))
    def _():
        for one, two in ((ext, halo), (ext2, halo2)):
            one[:, 0:HALF] = jnp.zeros((members, HALF, cols, levels), BF16)
            for side in range(2):
                two[side, :, 0] = jnp.zeros((members, HALF * HALF, levels), BF16)

    @pl.when(jnp.logical_not(has_down))
    def _():
        for one, two in ((ext, halo), (ext2, halo2)):
            one[:, rows + HALF : rows + 2 * HALF] = jnp.zeros((members, HALF, cols, levels), BF16)
            for side in range(2):
                two[side, :, groups + 1] = jnp.zeros((members, HALF * HALF, levels), BF16)

    with jax.named_scope("taps"):
        loads[4].wait()
        loads[5].wait()
    with jax.named_scope("filt"):
        filt[...] = filter_matrix(taps1, taps2, cols, False)
        border[...] = border_matrix(taps1, taps2, cols)

    first = iota((2 * HALF, levels), 0) < HALF

    def edges(block):
        tile = 2 * HALF
        near = [block[cols * r : cols * r + tile] for r in range(HALF)]
        far = [block[cols * (r + 1) - tile : cols * (r + 1)] for r in range(HALF)]
        lefts = [jnp.where(first, near[r], pltpu.roll(near[r + 1], HALF, 0)) for r in range(0, HALF, 2)]
        rights = [jnp.where(first, pltpu.roll(far[r], HALF, 0), far[r + 1]) for r in range(0, HALF, 2)]
        return jnp.concatenate(lefts, axis=0).astype(BF16), jnp.concatenate(rights, axis=0).astype(BF16)

    def pack_group(go, carry):
        for m in range(members):
            block = ext[m, pl.ds(HALF * (go + 1), HALF)].reshape(cells, levels).astype(F32)
            stage[0, m, go], stage[1, m, go] = edges(block)
        return carry

    with jax.named_scope("load0"):
        loads[0].wait()
    with jax.named_scope("pack"):
        lax.fori_loop(0, groups, pack_group, 0, unroll=4)

    half = chunks // 2
    tile = 2 * HALF
    loads[1].wait()
    v = vert[...].astype(F32)
    vt = v.T
    blank = jnp.zeros((levels, levels), F32)

    def diagonal(block):
        if width == 1:
            return block.astype(BF16)
        return jnp.concatenate(
            [jnp.concatenate([block, blank], axis=1), jnp.concatenate([blank, block], axis=1)], axis=0
        ).astype(BF16)

    vert2[...] = diagonal(v)
    vert2t[...] = diagonal(vt)
    sums[...] = jnp.zeros_like(sums)

    def tile_sum(x):
        return jnp.sum(x.reshape(-1, 8, levels), axis=0)

    def squares(go, carry):
        total = sums[...]
        for m in range(members):
            block = ext[m, pl.ds(HALF * (go + 1), HALF)].reshape(cells, levels).astype(F32)
            total = total + tile_sum(block * block)
        sums[...] = total
        return carry

    def smooth(source, sides, matrix, go, pair):
        blocks = []
        for m in pair:
            blocks.append(jnp.concatenate([
                source[m, pl.ds(HALF * go, 3 * HALF)].reshape(3 * cells, levels),
                sides[0, m, pl.ds(go, 3)].reshape(3 * HALF * HALF, levels),
                sides[1, m, pl.ds(go, 3)].reshape(3 * HALF * HALF, levels),
            ], axis=0))
        both = dot(matrix[...], jnp.concatenate(blocks, axis=1))
        return both[:cells] + both[cells:]

    pairs = [tuple(range(m, m + width)) for m in range(0, members, width)]

    def inner_rows(x):
        return jnp.concatenate([x[cols * r + tile : cols * (r + 1) - tile] for r in range(HALF)], axis=0)

    def rim_rows(x):
        ends = []
        for r in range(HALF):
            ends += [x[cols * r : cols * r + tile], x[cols * (r + 1) - tile : cols * (r + 1)]]
        return jnp.concatenate(ends, axis=0)

    def merge_rows(inner, rim):
        span = cols - 2 * tile
        blocks = []
        for r in range(HALF):
            blocks += [
                rim[2 * tile * r : 2 * tile * r + tile], inner[span * r : span * (r + 1)],
                rim[2 * tile * r + tile : 2 * tile * (r + 1)],
            ]
        return jnp.concatenate(blocks, axis=0)

    def spread_of(m, go):
        return ens[m, pl.ds(HALF * go, HALF)].reshape(cells, levels).astype(F32)

    def contribute(chunk, smoothed, pick, own, out, part):
        leveled = dot(jnp.concatenate(smoothed, axis=0), vert2[...])
        size = leveled.shape[0] // len(smoothed)
        at = 0
        for g in range(per):
            go = chunk * per + g
            total = None
            for pair in pairs:
                level = leveled[at : at + size]
                at += size
                for j, m in enumerate(pair):
                    term = pick(spread_of(m, go)) * level[:, j * levels : (j + 1) * levels]
                    total = term if total is None else total + term
            own[go] = total
            out[go] = total.astype(BF16)

    def forward_inner(chunk):
        smoothed = []
        for g in range(per):
            go = chunk * per + g
            for k, pair in enumerate(pairs):
                data = [ext[m, pl.ds(HALF * go, 3 * HALF)].reshape(3 * cells, levels) for m in pair]
                both = dot(filt[:, : 3 * cells], jnp.concatenate(data, axis=1))
                value = both[:cells] + both[cells:]
                keep[go, k] = rim_rows(value)
                smoothed.append(inner_rows(value).astype(BF16))
        contribute(chunk, smoothed, inner_rows, own_in, inner_out, 0)

    def forward_rim(chunk):
        smoothed = []
        for g in range(per):
            go = chunk * per + g
            for k, pair in enumerate(pairs):
                data = [
                    jnp.concatenate([
                        halo[0, m, pl.ds(go, 3)].reshape(3 * HALF * HALF, levels),
                        halo[1, m, pl.ds(go, 3)].reshape(3 * HALF * HALF, levels),
                    ], axis=0)
                    for m in pair
                ]
                both = dot(border[...], jnp.concatenate(data, axis=1))
                size = both.shape[0] // 2
                smoothed.append((keep[go, k] + both[:size] + both[size:]).astype(BF16))
        contribute(chunk, smoothed, rim_rows, own_rim, rim_out, 1)

    peers = n["mem"] - 1

    def weigh(chunk):
        for g in range(per):
            go = chunk * per + g
            inner, rim = own_in[go], own_rim[go]
            for peer in range(peers):
                inner = inner + inner_in[peer, go].astype(F32)
                rim = rim + rim_in[peer, go].astype(F32)
            increment = merge_rows(inner, rim)
            weighted = prec[pl.ds(HALF * go, HALF)].reshape(cells, levels) * increment
            sums[...] += tile_sum(weighted * increment) * (1.0 / n["mem"])
            wgt[go] = weighted

    def adjoint(chunk):
        places = [chunk * per + g for g in range(per)]
        rows_of = []
        for go in places:
            weighted = wgt[go]
            for pair in pairs:
                parts_of = []
                for m in pair:
                    parts_of.append((spread_of(m, go) * weighted).astype(BF16))
                rows_of.append(jnp.concatenate(parts_of, axis=1))
        result = dot(jnp.concatenate(rows_of, axis=0), vert2t[...])
        at = 0
        for go in places:
            for pair in pairs:
                for j, m in enumerate(pair):
                    block = result[at : at + cells, j * levels : (j + 1) * levels]
                    ext2[m, pl.ds(HALF * (go + 1), HALF)] = block.astype(BF16).reshape(HALF, cols, levels)
                    stage2[0, m, go], stage2[1, m, go] = edges(block)
                at += cells
        for copy in side_copies(1, stage2, halo2, chunk):
            copy.start()

    def final(chunk):
        for g in range(per):
            go = chunk * per + g
            for pair in pairs:
                back = smooth(ext2, halo2, filt2, go, pair)
                for j, m in enumerate(pair):
                    held = ext[m, pl.ds(HALF * (go + 1), HALF)].astype(F32)
                    block = back[:, j * levels : (j + 1) * levels].reshape(HALF, cols, levels)
                    hess[m, pl.ds(HALF * go, HALF)] = held + block

    def wait_sides(phase, src, dst, chunk):
        for copy in side_copies(phase, src, dst, chunk):
            copy.wait_recv()

    row2_up, row2_down = row_copies(
        1, ext2.at[:, pl.ds(HALF, HALF)], ext2.at[:, pl.ds(rows, HALF)], ext2
    )
    corner2_up, corner2_down = corner_copies(1, stage2, halo2)

    def here(at):
        return parts.at[place(at)], part_recv.at[place(at)]

    mine = device()
    part_out = [
        remote(here(mine)[0], here(mine)[0], part_send.at[k], here(mine)[1], ahead(step))
        for k, step in enumerate(steps)
    ]
    part_in = [
        remote(here(ahead(step))[0], here(ahead(step))[0], part_send.at[k], here(ahead(step))[1], ahead(step))
        for k, step in enumerate(steps)
    ]

    seen = {0: set(), 1: set()}

    def need_sides(phase, chunk):
        for at in (chunk - 1, chunk, chunk + 1):
            if 0 <= at < chunks and at not in seen[phase]:
                seen[phase].add(at)
                wait_sides(phase, *((stage, halo) if phase == 0 else (stage2, halo2)), at)

    row_up, row_down = row_copies(
        0, control.at[:, pl.ds(0, HALF)], control.at[:, pl.ds(rows - HALF, HALF)], ext
    )
    corner_up, corner_down = corner_copies(0, stage, halo)

    def start_inc(chunk, part):
        for copy in inc_copies(chunk, part):
            copy.start()

    def do_inner(chunk):
        if chunk == 0:
            with jax.named_scope("rowwait"):
                each(has_up, row_down + corner_down, "wait_recv")
        if chunk == chunks - 1:
            with jax.named_scope("rowwait"):
                each(has_down, row_up + corner_up, "wait_recv")
        with jax.named_scope("inner"):
            forward_inner(chunk)

    def do_rim(chunk):
        with jax.named_scope("rimwait"):
            need_sides(0, chunk)
        with jax.named_scope("rim"):
            forward_rim(chunk)
            start_inc(chunk, 1)

    adjointed, finished = set(), set()

    def do_adjoint(chunk):
        with jax.named_scope("incwait"):
            for part in range(2):
                for copy in inc_copies(chunk, part):
                    copy.wait_recv()
        with jax.named_scope("weigh"):
            weigh(chunk)
        adjointed.add(chunk)
        if len(adjointed) == chunks:
            with jax.named_scope("part"):
                parts[place(mine)] = jnp.sum(sums[...], axis=0, keepdims=True)
                for copy in part_out:
                    copy.start()
        with jax.named_scope("adj"):
            adjoint(chunk)
            if chunk == 0:
                each(has_up, row2_up + corner2_up, "start")
            if chunk == chunks - 1:
                each(has_down, row2_down + corner2_down, "start")

    def do_final(chunk):
        finished.add(chunk)
        with jax.named_scope("bwait"):
            need_sides(1, chunk)
            if chunk == 0:
                each(has_up, row2_down + corner2_down, "wait_recv")
            if chunk == chunks - 1:
                each(has_down, row2_up + corner2_up, "wait_recv")
        with jax.named_scope("fin"):
            final(chunk)

    middle = list(range(1, chunks - 1))
    early, late = middle[: half], middle[half:]
    with jax.named_scope("loads"):
        loads[2].wait()
    do_inner(middle[0])
    with jax.named_scope("barrier"):
        pl.semaphore_wait(barrier, len(steps))
    start_inc(middle[0], 0)
    for chunk in range(chunks):
        for copy in side_copies(0, stage, halo, chunk):
            copy.start()
    each(has_up, row_up + corner_up, "start")
    each(has_down, row_down + corner_down, "start")
    for chunk in middle[1:]:
        do_inner(chunk)
        start_inc(chunk, 0)
    with jax.named_scope("filt2"):
        filt2[...] = filter_matrix(taps1, taps2, cols, True)
    with jax.named_scope("squares"):
        lax.fori_loop(0, groups, squares, 0, unroll=2)
    loads[3].wait()
    for chunk in early:
        do_rim(chunk)
    for chunk in (0, chunks - 1):
        do_inner(chunk)
        start_inc(chunk, 0)
        do_rim(chunk)
    order = [*early, 0, chunks - 1, *late]
    at = 0
    for chunk in late:
        do_adjoint(order[at])
        at += 1
        do_rim(chunk)
    for position, now in enumerate(order):
        if position < at:
            continue
        do_adjoint(now)
        settled = order[:position]
        todo = [
            c for c in middle if c not in finished and all(d in settled for d in (c - 1, c, c + 1))
        ]
        if position < chunks - 1 and position > half - 1 and todo:
            do_final(todo[0])
    for chunk in middle:
        if chunk not in finished:
            do_final(chunk)
    do_final(chunks - 1)
    do_final(0)

    with jax.named_scope("redend"):
        for copy in part_in:
            copy.wait_recv()
        curv[0, 0] = jnp.sum(parts[...]) * (1.0 / entries)

    with jax.named_scope("finish"):
        for copy in part_out:
            copy.wait_send()
        each(has_up, row_up + corner_up + row2_up + corner2_up, "wait_send")
        each(has_down, row_down + corner_down + row2_down + corner2_down, "wait_send")

        def finish(chunk, carry):
            for copy in side_copies(0, stage, halo, chunk) + side_copies(1, stage2, halo2, chunk):
                copy.wait_send()
            for copy in inc_copies(chunk, 0) + inc_copies(chunk, 1):
                copy.wait_send()
            return carry

        lax.fori_loop(0, chunks, finish, 0)


def per_device(axes, sizes, control, ensemble, precision, lat_taps, lon_taps, vertical):
    members, rows, cols, levels = control.shape
    n = dict(zip(axes, sizes))
    groups = rows // HALF
    cells = HALF * cols
    pack = HALF * HALF
    entries = control.size
    for size in sizes:
        entries *= size
    chunks = next(c for c in (8, 4, groups) if groups % c == 0)
    width = 2 if members % 2 == 0 else 1
    inner = 3 * cells + 6 * pack
    rim = 4 * pack
    smem = pl.BlockSpec(memory_space=pltpu.SMEM)
    anyspace = pl.BlockSpec(memory_space=pltpu.HBM)
    peers = max(n["mem"] - 1, 1)
    hessian, curvature = pl.pallas_call(
        functools.partial(kernel, axes, sizes, entries, chunks),
        out_shape=(
            pltpu.VMEM(control.shape, F32),
            jax.ShapeDtypeStruct((1, 1), F32),
        ),
        in_specs=[anyspace, anyspace, anyspace, anyspace, anyspace, anyspace],
        out_specs=(pl.BlockSpec(memory_space=pltpu.VMEM), smem),
        scratch_shapes=[
            pltpu.VMEM((members, rows + 2 * HALF, cols, levels), BF16),
            pltpu.VMEM((members, rows + 2 * HALF, cols, levels), BF16),
            pltpu.VMEM(control.shape, BF16),
            pltpu.VMEM(precision.shape, F32),
            pltpu.VMEM((groups, cells - rim, levels), F32),
            pltpu.VMEM((groups, rim, levels), F32),
            pltpu.VMEM((groups, cells, levels), F32),
            pltpu.VMEM((groups, cells - rim, levels), BF16),
            pltpu.VMEM((groups, rim, levels), BF16),
            pltpu.VMEM((peers, groups, cells - rim, levels), BF16),
            pltpu.VMEM((peers, groups, rim, levels), BF16),
            pltpu.VMEM((groups, members // width, rim, width * levels), F32),
            pltpu.VMEM((2, members, groups + 2, pack, levels), BF16),
            pltpu.VMEM((2, members, groups + 2, pack, levels), BF16),
            pltpu.VMEM((2, members, groups, pack, levels), BF16),
            pltpu.VMEM((2, members, groups, pack, levels), BF16),
            pltpu.VMEM((2 * cells, inner), BF16),
            pltpu.VMEM((2 * cells, inner), BF16),
            pltpu.VMEM((2 * rim, 6 * pack), BF16),
            pltpu.VMEM((levels, levels), BF16),
            pltpu.VMEM((width * levels, width * levels), BF16),
            pltpu.VMEM((width * levels, width * levels), BF16),
            pltpu.VMEM((8, levels), F32),
            pltpu.VMEM((math.prod(sizes), 1, levels), F32),
            pltpu.SMEM(lat_taps.shape, F32),
            pltpu.SMEM(lon_taps.shape, F32),
            pltpu.SemaphoreType.DMA((6,)),
            pltpu.SemaphoreType.DMA((2, 6)),
            pltpu.SemaphoreType.DMA((2, 6)),
            pltpu.SemaphoreType.DMA((2, 2, chunks)),
            pltpu.SemaphoreType.DMA((2, 2, chunks)),
            pltpu.SemaphoreType.DMA((2, peers, chunks)),
            pltpu.SemaphoreType.DMA((2, peers, chunks)),
            pltpu.SemaphoreType.DMA((math.prod(sizes),)),
            pltpu.SemaphoreType.DMA((math.prod(sizes),)),
        ],
        compiler_params=pltpu.CompilerParams(
            collective_id=0, has_side_effects=True, vmem_limit_bytes=59 * 1024 * 1024
        ),
    )(lat_taps, lon_taps, control, ensemble, precision, vertical)
    return hessian, curvature.reshape(())


def solution(mesh):
    axes = tuple(mesh.axis_names)
    sizes = tuple(mesh.shape[a] for a in axes)
    in_specs = (
        P("mem", "lat", "lon", None),
        P("mem", "lat", "lon", None),
        P("lat", "lon", None),
        P(),
        P(),
        P(),
    )
    out_specs = (P("mem", "lat", "lon", None), P())
    return jax.shard_map(
        functools.partial(per_device, axes, sizes),
        mesh=mesh, in_specs=in_specs, out_specs=out_specs, check_vma=False,
    )
```

```python
import functools
import itertools
import math

import jax
import jax.numpy as jnp
from jax import lax
from jax.experimental import pallas as pl
from jax.experimental.pallas import tpu as pltpu
from jax.sharding import PartitionSpec as P

F32 = jnp.float32
BF16 = jnp.bfloat16
HALF = 4


def iota(shape, dim):
    return lax.broadcasted_iota(jnp.int32, shape, dim)


def tap_products(lat_taps, lon_taps, down, across, reverse):
    taps = lat_taps.shape[0]
    first = jnp.zeros(down.shape, F32)
    second = jnp.zeros(down.shape, F32)
    for tap in range(taps):
        at = taps - 1 - tap if reverse else tap
        first = jnp.where(down == tap, lat_taps[at], first)
        second = jnp.where(across == tap, lon_taps[at], second)
    full = first * second
    high = full.astype(BF16)
    low = (full - high.astype(F32)).astype(BF16)
    return jnp.concatenate([high, low], axis=0)


def full_matrix(lat_taps, lon_taps, cols, reverse):
    shape = (HALF * cols, 3 * HALF * cols + 6 * HALF * HALF)
    out, src = iota(shape, 0), iota(shape, 1)
    main = 3 * HALF * cols
    side = 3 * HALF * HALF
    inside = src < main
    left = src < main + side
    packed = jnp.where(left, src - main, src - main - side)
    row = jnp.where(inside, src // cols, packed // HALF)
    col = jnp.where(
        inside, src % cols, packed % HALF + jnp.where(left, -HALF, cols)
    )
    return tap_products(lat_taps, lon_taps, row - out // cols, col - out % cols + HALF, reverse)


def inner_matrix(lat_taps, lon_taps, cols, reverse):
    span = cols - 4 * HALF
    shape = (HALF * span, 3 * HALF * cols)
    out, src = iota(shape, 0), iota(shape, 1)
    down = src // cols - out // span
    across = src % cols - (out % span + 2 * HALF) + HALF
    return tap_products(lat_taps, lon_taps, down, across, reverse)


def rim_matrix(lat_taps, lon_taps, side, reverse):
    tile = 2 * HALF
    main = 3 * HALF * 2 * tile
    shape = (HALF * tile, main + 3 * HALF * HALF)
    out, src = iota(shape, 0), iota(shape, 1)
    inside = src < main
    packed = src - main
    row = jnp.where(inside, src // (2 * tile), packed // HALF)
    col = jnp.where(inside, src % (2 * tile), packed % HALF + (2 * tile if side else -HALF))
    down = row - out // tile
    across = col - (out % tile + (tile if side else 0)) + HALF
    return tap_products(lat_taps, lon_taps, down, across, reverse)


def dot(a, b):
    return jnp.dot(a, b, preferred_element_type=F32)


def kernel(
    axes, sizes, entries, chunks, lat_taps, lon_taps, control, ensemble, precision, vertical, hess, curv,
    ext, ext2, ens, prec, own_in, own_rim, wgt, inner_out, rim_out, inner_in, rim_in, halo, halo2, stage, stage2,
    mid, near, far, filt2, vert, vert2, vert2t, sums, parts, taps1, taps2,
    local_sem, row_send, row_recv, corner_send, corner_recv, side_send, side_recv, inc_send, inc_recv, part_sem, met,
):
    members, rows, cols, levels = control.shape
    groups = rows // HALF
    per = groups // chunks
    cells = HALF * cols
    width = 2 if members % 2 == 0 else 1
    me = {a: lax.axis_index(a) for a in axes}
    n = dict(zip(axes, sizes))

    def device(**at):
        return tuple(at.get(a, me[a]) for a in axes)

    def place(to):
        index = 0
        for size, at in zip(sizes, to):
            index = index * size + at
        return index

    lat, lon = me["lat"], me["lon"]
    left = lax.rem(lon + n["lon"] - 1, n["lon"])
    right = lax.rem(lon + 1, n["lon"])
    has_up = lat > 0
    has_down = lat < n["lat"] - 1
    steps = [s for s in itertools.product(*(range(size) for size in sizes)) if any(s)]

    def ahead(step):
        return tuple(lax.rem(me[a] + d, n[a]) if d else me[a] for a, d in zip(axes, step))

    deep = per * HALF
    head, tail = pl.ds(0, 3 * deep), pl.ds(3 * deep, rows - 3 * deep)
    front, back_rows = pl.ds(deep, deep), pl.ds(2 * deep, rows - 2 * deep)
    loads = [
        pltpu.make_async_copy(control.at[:, head], ext.at[:, pl.ds(HALF, 3 * deep)], local_sem.at[0]),
        pltpu.make_async_copy(vertical, vert, local_sem.at[1]),
        pltpu.make_async_copy(ensemble.at[:, front], ens.at[:, front], local_sem.at[2]),
        pltpu.make_async_copy(ensemble.at[:, back_rows], ens.at[:, back_rows], local_sem.at[3]),
        pltpu.make_async_copy(lat_taps, taps1, local_sem.at[4]),
        pltpu.make_async_copy(lon_taps, taps2, local_sem.at[5]),
        pltpu.make_async_copy(ensemble.at[:, pl.ds(0, deep)], ens.at[:, pl.ds(0, deep)], local_sem.at[6]),
        pltpu.make_async_copy(precision, prec, local_sem.at[7]),
        pltpu.make_async_copy(
            control.at[:, tail], ext.at[:, pl.ds(HALF + 3 * deep, rows - 3 * deep)], local_sem.at[8]
        ),
    ]
    for at in (4, 5, 0, 2, 1, 8, 3, 6, 7):
        loads[at].start()

    barrier = pltpu.get_barrier_semaphore()
    plane = [s for s in steps if not s[axes.index("lat")]]

    def signal(semaphore, to):
        pl.semaphore_signal(semaphore, inc=1, device_id=to, device_id_type=pl.DeviceIdType.MESH)

    for step in plane:
        signal(barrier, ahead(step))
    for has, row in ((has_up, lat - 1), (has_down, lat + 1)):
        @pl.when(has)
        def _():
            for col in (lon, left, right):
                signal(barrier, device(lat=row, lon=col))
    beside = jnp.where(has_up, 1, 0) + jnp.where(has_down, 1, 0)

    def hello(turn):
        for has, row in ((has_up, lat - 1), (has_down, lat + 1)):
            @pl.when(has)
            def _():
                signal(met.at[turn], device(lat=row))

    def hear(turn):
        pl.semaphore_wait(met.at[turn], beside)

    def remote(src, dst, send, recv, to):
        return pltpu.make_async_remote_copy(
            src_ref=src, dst_ref=dst, send_sem=send, recv_sem=recv,
            device_id=to, device_id_type=pl.DeviceIdType.MESH,
        )

    def row_copies(phase, up_src, down_src, dst):
        up = remote(
            up_src, dst.at[:, pl.ds(rows + HALF, HALF)],
            row_send.at[phase, 0], row_recv.at[phase, 0], device(lat=lat - 1),
        )
        down = remote(
            down_src, dst.at[:, pl.ds(0, HALF)],
            row_send.at[phase, 1], row_recv.at[phase, 1], device(lat=lat + 1),
        )
        return [up], [down]

    def corner_copies(phase, src, dst):
        up, down = [], []
        for side, to in ((0, left), (1, right)):
            there = dst.at[1 - side]
            mine = src.at[side]
            up.append(remote(
                mine.at[:, 0], there.at[:, groups + 1],
                corner_send.at[phase, 0], corner_recv.at[phase, 0], device(lat=lat - 1, lon=to),
            ))
            down.append(remote(
                mine.at[:, groups - 1], there.at[:, 0],
                corner_send.at[phase, 1], corner_recv.at[phase, 1], device(lat=lat + 1, lon=to),
            ))
        return up, down

    def corner_waits(phase, src, dst):
        up = remote(
            src.at[:, :, 0], dst.at[:, :, groups + 1],
            corner_send.at[phase, 0], corner_recv.at[phase, 0], device(lat=lat - 1, lon=left),
        )
        down = remote(
            src.at[:, :, groups - 1], dst.at[:, :, 0],
            corner_send.at[phase, 1], corner_recv.at[phase, 1], device(lat=lat + 1, lon=left),
        )
        return [up], [down]

    def side_copies(phase, src, dst, chunk):
        return [
            remote(
                src.at[side, :, pl.ds(chunk * per, per)], dst.at[1 - side, :, pl.ds(chunk * per + 1, per)],
                side_send.at[phase], side_recv.at[phase, chunk], device(lon=to),
            )
            for side, to in ((0, left), (1, right))
        ]

    def side_arrival(phase, src, dst, chunk):
        return remote(
            src.at[:, :, pl.ds(chunk * per, per)], dst.at[:, :, pl.ds(chunk * per + 1, per)],
            side_send.at[phase], side_recv.at[phase, chunk], device(lon=left),
        )

    def inc_copies(chunk, part):
        at = pl.ds(chunk * per, per)
        out, into = ((inner_out, inner_in), (rim_out, rim_in))[part]
        return [
            remote(
                out.at[at], into.at[step - 1, at],
                inc_send.at[part, step - 1], inc_recv.at[part, step - 1, chunk],
                device(mem=lax.rem(me["mem"] + step, n["mem"])),
            )
            for step in range(1, n["mem"])
        ]

    def each(has, copies, act):
        @pl.when(has)
        def _():
            for copy in copies:
                getattr(copy, act)()

    @pl.when(jnp.logical_not(has_up))
    def _():
        for one, two in ((ext, halo), (ext2, halo2)):
            one[:, 0:HALF] = jnp.zeros((members, HALF, cols, levels), BF16)
            for side in range(2):
                two[side, :, 0] = jnp.zeros((members, HALF * HALF, levels), BF16)

    @pl.when(jnp.logical_not(has_down))
    def _():
        for one, two in ((ext, halo), (ext2, halo2)):
            one[:, rows + HALF : rows + 2 * HALF] = jnp.zeros((members, HALF, cols, levels), BF16)
            for side in range(2):
                two[side, :, groups + 1] = jnp.zeros((members, HALF * HALF, levels), BF16)

    with jax.named_scope("taps"):
        loads[4].wait()
        loads[5].wait()
    with jax.named_scope("filt"):
        mid[...] = inner_matrix(taps1, taps2, cols, False)

    first = iota((2 * HALF, levels), 0) < HALF

    def edges(block):
        tile = 2 * HALF
        near = [block[cols * r : cols * r + tile] for r in range(HALF)]
        far = [block[cols * (r + 1) - tile : cols * (r + 1)] for r in range(HALF)]
        lefts = [jnp.where(first, near[r], pltpu.roll(near[r + 1], HALF, 0)) for r in range(0, HALF, 2)]
        rights = [jnp.where(first, pltpu.roll(far[r], HALF, 0), far[r + 1]) for r in range(0, HALF, 2)]
        return jnp.concatenate(lefts, axis=0).astype(BF16), jnp.concatenate(rights, axis=0).astype(BF16)

    def pack_group(go, carry):
        for m in range(members):
            block = ext[m, pl.ds(HALF * (go + 1), HALF)].reshape(cells, levels).astype(F32)
            stage[0, m, go], stage[1, m, go] = edges(block)
        return carry

    half = chunks // 2
    tile = 2 * HALF
    loads[1].wait()
    v = vert[...].astype(F32)
    vt = v.T
    blank = jnp.zeros((levels, levels), F32)

    def diagonal(block):
        if width == 1:
            return block.astype(BF16)
        return jnp.concatenate(
            [jnp.concatenate([block, blank], axis=1), jnp.concatenate([blank, block], axis=1)], axis=0
        ).astype(BF16)

    vert2[...] = diagonal(v)
    vert2t[...] = diagonal(vt)
    sums[...] = jnp.zeros_like(sums)

    def tile_sum(x):
        return jnp.sum(x.reshape(-1, 8, levels), axis=0)

    def squares(go, carry):
        total = sums[...]
        for m in range(members):
            block = ext[m, pl.ds(HALF * (go + 1), HALF)].reshape(cells, levels).astype(F32)
            total = total + tile_sum(block * block)
        sums[...] = total
        return carry

    def halves(matrix, data):
        both = dot(matrix[...], data)
        size = both.shape[0] // 2
        return both[:size] + both[size:]

    def smooth_inner(source, matrix, go, pair):
        data = [source[m, pl.ds(HALF * go, 3 * HALF)].reshape(3 * cells, levels) for m in pair]
        return halves(matrix, jnp.concatenate(data, axis=1))

    def smooth_rim(source, sides, matrices, go, pair):
        ends = []
        for side, matrix in enumerate(matrices):
            data = [
                jnp.concatenate([
                    source[m, pl.ds(HALF * go, 3 * HALF), (cols - 2 * tile) * side : (cols - 2 * tile) * side + 2 * tile]
                    .reshape(3 * HALF * 2 * tile, levels),
                    sides[side, m, pl.ds(go, 3)].reshape(3 * HALF * HALF, levels),
                ], axis=0)
                for m in pair
            ]
            ends.append(halves(matrix, jnp.concatenate(data, axis=1)))
        return jnp.concatenate(ends, axis=0)

    pairs = [tuple(range(m, m + width)) for m in range(0, members, width)]

    def inner_rows(x):
        return jnp.concatenate([x[cols * r + tile : cols * (r + 1) - tile] for r in range(HALF)], axis=0)

    def rim_rows(x):
        lefts = [x[cols * r : cols * r + tile] for r in range(HALF)]
        rights = [x[cols * (r + 1) - tile : cols * (r + 1)] for r in range(HALF)]
        return jnp.concatenate(lefts + rights, axis=0)

    def merge_rows(inner, rim):
        span = cols - 2 * tile
        blocks = []
        for r in range(HALF):
            blocks += [
                rim[tile * r : tile * (r + 1)], inner[span * r : span * (r + 1)],
                rim[tile * (HALF + r) : tile * (HALF + r + 1)],
            ]
        return jnp.concatenate(blocks, axis=0)

    def spread_of(m, go):
        return ens[m, pl.ds(HALF * go, HALF)].reshape(cells, levels).astype(F32)

    def contribute(places, smoothed, pick, own, out):
        leveled = dot(jnp.concatenate(smoothed, axis=0), vert2[...])
        size = leveled.shape[0] // len(smoothed)
        at = 0
        for go in places:
            total = None
            for pair in pairs:
                level = leveled[at : at + size]
                at += size
                for j, m in enumerate(pair):
                    term = pick(spread_of(m, go)) * level[:, j * levels : (j + 1) * levels]
                    total = term if total is None else total + term
            own[go] = total
            out[go] = total.astype(BF16)

    def places_of(chunk):
        return [chunk * per + g for g in range(per)]

    def forward_inner(chunk):
        places = places_of(chunk)
        smoothed = [smooth_inner(ext, mid, go, pair).astype(BF16) for go in places for pair in pairs]
        contribute(places, smoothed, inner_rows, own_in, inner_out)

    def forward_rim(some):
        places = [go for chunk in some for go in places_of(chunk)]
        smoothed = [smooth_rim(ext, halo, (near, far), go, pair).astype(BF16) for go in places for pair in pairs]
        contribute(places, smoothed, rim_rows, own_rim, rim_out)

    peers = n["mem"] - 1

    def weigh(chunk):
        for g in range(per):
            go = chunk * per + g
            inner, rim = own_in[go], own_rim[go]
            for peer in range(peers):
                inner = inner + inner_in[peer, go].astype(F32)
                rim = rim + rim_in[peer, go].astype(F32)
            increment = merge_rows(inner, rim)
            weighted = prec[pl.ds(HALF * go, HALF)].reshape(cells, levels) * increment
            sums[...] += tile_sum(weighted * increment) * (1.0 / n["mem"])
            wgt[go] = weighted

    def adjoint(chunk):
        places = [chunk * per + g for g in range(per)]
        rows_of = []
        for go in places:
            weighted = wgt[go]
            for pair in pairs:
                parts_of = []
                for m in pair:
                    parts_of.append((spread_of(m, go) * weighted).astype(BF16))
                rows_of.append(jnp.concatenate(parts_of, axis=1))
        result = dot(jnp.concatenate(rows_of, axis=0), vert2t[...])
        at = 0
        for go in places:
            for pair in pairs:
                for j, m in enumerate(pair):
                    block = result[at : at + cells, j * levels : (j + 1) * levels]
                    ext2[m, pl.ds(HALF * (go + 1), HALF)] = block.astype(BF16).reshape(HALF, cols, levels)
                    stage2[0, m, go], stage2[1, m, go] = edges(block)
                at += cells
        for copy in side_copies(1, stage2, halo2, chunk):
            copy.start()

    def smooth(source, sides, matrix, go, pair):
        data = [
            jnp.concatenate([
                source[m, pl.ds(HALF * go, 3 * HALF)].reshape(3 * cells, levels),
                sides[0, m, pl.ds(go, 3)].reshape(3 * HALF * HALF, levels),
                sides[1, m, pl.ds(go, 3)].reshape(3 * HALF * HALF, levels),
            ], axis=0)
            for m in pair
        ]
        return halves(matrix, jnp.concatenate(data, axis=1))

    def final(chunk):
        for go in places_of(chunk):
            for pair in pairs:
                back = smooth(ext2, halo2, filt2, go, pair)
                for j, m in enumerate(pair):
                    held = ext[m, pl.ds(HALF * (go + 1), HALF)].astype(F32)
                    block = back[:, j * levels : (j + 1) * levels].reshape(HALF, cols, levels)
                    hess[m, pl.ds(HALF * go, HALF)] = held + block

    def wait_sides(phase, src, dst, chunk):
        side_arrival(phase, src, dst, chunk).wait_recv()

    row2_up, row2_down = row_copies(
        1, ext2.at[:, pl.ds(HALF, HALF)], ext2.at[:, pl.ds(rows, HALF)], ext2
    )
    corner2_up, corner2_down = corner_copies(1, stage2, halo2)
    both2_up, both2_down = corner_waits(1, stage2, halo2)

    mine = place(device())
    part_out = [remote(parts.at[mine], parts.at[mine], part_sem.at[0], part_sem.at[1], ahead(step)) for step in steps]
    others = parts.at[pl.ds(0, len(steps))]
    part_all = remote(others, others, part_sem.at[0], part_sem.at[1], ahead(steps[0]))

    seen = {0: set(), 1: set()}

    def need_sides(phase, chunk):
        for at in (chunk - 1, chunk, chunk + 1):
            if 0 <= at < chunks and at not in seen[phase]:
                seen[phase].add(at)
                wait_sides(phase, *((stage, halo) if phase == 0 else (stage2, halo2)), at)

    row_up, row_down = row_copies(
        0, control.at[:, pl.ds(0, HALF)], control.at[:, pl.ds(rows - HALF, HALF)], ext
    )
    corner_up, corner_down = corner_copies(0, stage, halo)
    both_up, both_down = corner_waits(0, stage, halo)

    def start_inc(chunk, part):
        for copy in inc_copies(chunk, part):
            copy.start()

    def do_inner(chunk):
        if chunk == 0:
            with jax.named_scope("rowwait"):
                each(has_up, row_down + both_down, "wait_recv")
        if chunk == chunks - 1:
            with jax.named_scope("rowwait"):
                each(has_down, row_up + both_up, "wait_recv")
        with jax.named_scope("inner"):
            forward_inner(chunk)

    def do_rim(*some):
        with jax.named_scope("rimwait"):
            for chunk in some:
                need_sides(0, chunk)
        with jax.named_scope("rim"):
            forward_rim(some)
            for chunk in some:
                start_inc(chunk, 1)

    adjointed = set()

    def do_adjoint(chunk):
        with jax.named_scope("incwait"):
            for part in range(2):
                for copy in inc_copies(chunk, part):
                    copy.wait_recv()
        with jax.named_scope("weigh"):
            weigh(chunk)
        adjointed.add(chunk)
        if len(adjointed) == chunks:
            with jax.named_scope("part"):
                parts[mine] = jnp.sum(sums[...], axis=0, keepdims=True)
                for copy in part_out:
                    copy.start()
        with jax.named_scope("adj"):
            adjoint(chunk)
            if chunk == 0:
                each(has_up, row2_up + corner2_up, "start")
            if chunk == chunks - 1:
                each(has_down, row2_down + corner2_down, "start")

    def do_final(chunk):
        with jax.named_scope("bwait"):
            need_sides(1, chunk)
            if chunk == 0:
                each(has_up, row2_down + both2_down, "wait_recv")
            if chunk == chunks - 1:
                each(has_down, row2_up + both2_up, "wait_recv")
        with jax.named_scope("fin"):
            final(chunk)

    middle = list(range(1, chunks - 1))
    turns = n["lat"] - 1
    with jax.named_scope("load0"):
        loads[0].wait()
        loads[2].wait()
    do_inner(middle[0])
    with jax.named_scope("barrier"):
        pl.semaphore_wait(barrier, len(plane) + 3 * beside)
    start_inc(middle[0], 0)
    each(has_up, row_up, "start")
    each(has_down, row_down, "start")
    with jax.named_scope("load8"):
        loads[8].wait()
    with jax.named_scope("pack"):
        lax.fori_loop(0, groups, pack_group, 0, unroll=4)
    for chunk in range(chunks):
        for copy in side_copies(0, stage, halo, chunk):
            copy.start()
        if chunk == half:
            each(has_up, corner_up, "start")
            each(has_down, corner_down, "start")
    met_turns = []

    def meet():
        turn = len(met_turns)
        if turn > turns:
            return
        met_turns.append(turn)
        with jax.named_scope("meet"):
            if turn > 0:
                hear(turn - 1)
            if turn < turns:
                hello(turn)

    meet()
    with jax.named_scope("load3"):
        loads[3].wait()
        loads[6].wait()
    for chunk in middle[1:]:
        do_inner(chunk)
        start_inc(chunk, 0)
        if chunk == middle[half - 1]:
            meet()
    with jax.named_scope("filt2"):
        near[...] = rim_matrix(taps1, taps2, 0, False)
        far[...] = rim_matrix(taps1, taps2, 1, False)
        filt2[...] = full_matrix(taps1, taps2, cols, True)
    with jax.named_scope("squares"):
        lax.fori_loop(0, groups, squares, 0, unroll=2)
    with jax.named_scope("load7"):
        loads[7].wait()
    last = chunks - 1
    lead = middle[: half - 1]
    rest = [c for c in middle if c not in lead and c != last - 1]
    batches = [lead[:1], lead[1:], [0], *[[c] for c in rest], [last, last - 1]]
    order = [c for batch in batches for c in batch]
    at = 0
    for index, batch in enumerate(batches):
        if batch:
            do_rim(*batch)
        if index == 0:
            for chunk in (0, last):
                do_inner(chunk)
                start_inc(chunk, 0)
        if index == 1:
            meet()
        if index >= 2 and index % 2 == 0 and at < len(order) - 2:
            do_adjoint(order[at])
            at += 1
    for position, now in enumerate(order):
        if position < at:
            continue
        if position == chunks - 2:
            while len(met_turns) <= turns:
                meet()
        do_adjoint(now)
    for chunk in middle:
        do_final(chunk)
    do_final(last)
    do_final(0)

    with jax.named_scope("redend"):
        part_all.wait_recv()
        curv[0, 0] = jnp.sum(parts[...]) * (1.0 / entries)

    with jax.named_scope("finish"):
        part_all.wait_send()
        each(has_up, row_up + both_up + row2_up + both2_up, "wait_send")
        each(has_down, row_down + both_down + row2_down + both2_down, "wait_send")
        for phase, src, dst in ((0, stage, halo), (1, stage2, halo2)):
            remote(src, dst.at[:, :, pl.ds(1, groups)], side_send.at[phase], side_recv.at[phase, 0], device(lon=left)).wait_send()
        for part, out, into in ((0, inner_out, inner_in), (1, rim_out, rim_in)):
            for step in range(1, n["mem"]):
                remote(
                    out, into.at[step - 1], inc_send.at[part, step - 1], inc_recv.at[part, step - 1, 0],
                    device(mem=lax.rem(me["mem"] + step, n["mem"])),
                ).wait_send()


def per_device(axes, sizes, control, ensemble, precision, lat_taps, lon_taps, vertical):
    members, rows, cols, levels = control.shape
    n = dict(zip(axes, sizes))
    groups = rows // HALF
    cells = HALF * cols
    pack = HALF * HALF
    entries = control.size
    for size in sizes:
        entries *= size
    chunks = next(c for c in (8, 4, groups) if groups % c == 0)
    width = 2 if members % 2 == 0 else 1
    rim = 4 * pack
    smem = pl.BlockSpec(memory_space=pltpu.SMEM)
    anyspace = pl.BlockSpec(memory_space=pltpu.HBM)
    peers = max(n["mem"] - 1, 1)
    hessian, curvature = pl.pallas_call(
        functools.partial(kernel, axes, sizes, entries, chunks),
        out_shape=(
            pltpu.VMEM(control.shape, F32),
            jax.ShapeDtypeStruct((1, 1), F32),
        ),
        in_specs=[anyspace, anyspace, anyspace, anyspace, anyspace, anyspace],
        out_specs=(pl.BlockSpec(memory_space=pltpu.VMEM), smem),
        scratch_shapes=[
            pltpu.VMEM((members, rows + 2 * HALF, cols, levels), BF16),
            pltpu.VMEM((members, rows + 2 * HALF, cols, levels), BF16),
            pltpu.VMEM(control.shape, BF16),
            pltpu.VMEM(precision.shape, F32),
            pltpu.VMEM((groups, cells - rim, levels), F32),
            pltpu.VMEM((groups, rim, levels), F32),
            pltpu.VMEM((groups, cells, levels), F32),
            pltpu.VMEM((groups, cells - rim, levels), BF16),
            pltpu.VMEM((groups, rim, levels), BF16),
            pltpu.VMEM((peers, groups, cells - rim, levels), BF16),
            pltpu.VMEM((peers, groups, rim, levels), BF16),
            pltpu.VMEM((2, members, groups + 2, pack, levels), BF16),
            pltpu.VMEM((2, members, groups + 2, pack, levels), BF16),
            pltpu.VMEM((2, members, groups, pack, levels), BF16),
            pltpu.VMEM((2, members, groups, pack, levels), BF16),
            pltpu.VMEM((2 * (cells - rim), 3 * cells), BF16),
            pltpu.VMEM((rim, 15 * pack), BF16),
            pltpu.VMEM((rim, 15 * pack), BF16),
            pltpu.VMEM((2 * cells, 3 * cells + 6 * pack), BF16),
            pltpu.VMEM((levels, levels), BF16),
            pltpu.VMEM((width * levels, width * levels), BF16),
            pltpu.VMEM((width * levels, width * levels), BF16),
            pltpu.VMEM((8, levels), F32),
            pltpu.VMEM((math.prod(sizes), 1, levels), F32),
            pltpu.SMEM(lat_taps.shape, F32),
            pltpu.SMEM(lon_taps.shape, F32),
            pltpu.SemaphoreType.DMA((9,)),
            pltpu.SemaphoreType.DMA((2, 2)),
            pltpu.SemaphoreType.DMA((2, 2)),
            pltpu.SemaphoreType.DMA((2, 2)),
            pltpu.SemaphoreType.DMA((2, 2)),
            pltpu.SemaphoreType.DMA((2,)),
            pltpu.SemaphoreType.DMA((2, chunks)),
            pltpu.SemaphoreType.DMA((2, peers)),
            pltpu.SemaphoreType.DMA((2, peers, chunks)),
            pltpu.SemaphoreType.DMA((2,)),
            pltpu.SemaphoreType.REGULAR((max(n["lat"] - 1, 1),)),
        ],
        compiler_params=pltpu.CompilerParams(
            collective_id=0, has_side_effects=True, vmem_limit_bytes=59 * 1024 * 1024
        ),
    )(lat_taps, lon_taps, control, ensemble, precision, vertical)
    return hessian, curvature.reshape(())


def solution(mesh):
    axes = tuple(mesh.axis_names)
    sizes = tuple(mesh.shape[a] for a in axes)
    in_specs = (
        P("mem", "lat", "lon", None),
        P("mem", "lat", "lon", None),
        P("lat", "lon", None),
        P(),
        P(),
        P(),
    )
    out_specs = (P("mem", "lat", "lon", None), P())
    return jax.shard_map(
        functools.partial(per_device, axes, sizes),
        mesh=mesh, in_specs=in_specs, out_specs=out_specs, check_vma=False,
    )
```

```python
import functools
import itertools

import jax
import jax.numpy as jnp
from jax import lax
from jax.experimental import pallas as pl
from jax.experimental.pallas import tpu as pltpu
from jax.sharding import PartitionSpec as P

F32 = jnp.float32
BF16 = jnp.bfloat16
HALF = 4


def iota(shape, dim):
    return lax.broadcasted_iota(jnp.int32, shape, dim)


def tap_products(lat_taps, lon_taps, down, across, reverse):
    taps = lat_taps.shape[0]
    first = jnp.zeros(down.shape, F32)
    second = jnp.zeros(down.shape, F32)
    for tap in range(taps):
        at = taps - 1 - tap if reverse else tap
        first = jnp.where(down == tap, lat_taps[at], first)
        second = jnp.where(across == tap, lon_taps[at], second)
    full = first * second
    high = full.astype(BF16)
    low = (full - high.astype(F32)).astype(BF16)
    return jnp.concatenate([high, low], axis=0)


def full_matrix(lat_taps, lon_taps, cols, reverse):
    shape = (HALF * cols, 3 * HALF * cols + 6 * HALF * HALF)
    out, src = iota(shape, 0), iota(shape, 1)
    main = 3 * HALF * cols
    side = 3 * HALF * HALF
    inside = src < main
    left = src < main + side
    packed = jnp.where(left, src - main, src - main - side)
    row = jnp.where(inside, src // cols, packed // HALF)
    col = jnp.where(
        inside, src % cols, packed % HALF + jnp.where(left, -HALF, cols)
    )
    return tap_products(lat_taps, lon_taps, row - out // cols, col - out % cols + HALF, reverse)


def inner_matrix(lat_taps, lon_taps, cols, reverse):
    span = cols - 4 * HALF
    shape = (HALF * span, 3 * HALF * cols)
    out, src = iota(shape, 0), iota(shape, 1)
    down = src // cols - out // span
    across = src % cols - (out % span + 2 * HALF) + HALF
    return tap_products(lat_taps, lon_taps, down, across, reverse)


def rim_matrix(lat_taps, lon_taps, side, reverse):
    tile = 2 * HALF
    main = 3 * HALF * 2 * tile
    shape = (HALF * tile, main + 3 * HALF * HALF)
    out, src = iota(shape, 0), iota(shape, 1)
    inside = src < main
    packed = src - main
    row = jnp.where(inside, src // (2 * tile), packed // HALF)
    col = jnp.where(inside, src % (2 * tile), packed % HALF + (2 * tile if side else -HALF))
    down = row - out // tile
    across = col - (out % tile + (tile if side else 0)) + HALF
    return tap_products(lat_taps, lon_taps, down, across, reverse)


def dot(a, b):
    return jnp.dot(a, b, preferred_element_type=F32)


def kernel(
    axes, sizes, entries, chunks, lat_taps, lon_taps, control, ensemble, precision, vertical, hess, curv,
    ext, ext2, ens, prec, wgt, inners, rims, halo, halo2, stage, stage2,
    mid, near, far, filt2, vert, vert2, vert2t, sums, parts, norms, taps1, taps2,
    local_sem, row_send, row_recv, corner_send, corner_recv, side_send, side_recv, inc_send, inc_recv, part_sem, norm_send, norm_recv, met,
):
    members, rows, cols, levels = control.shape
    groups = rows // HALF
    per = groups // chunks
    cells = HALF * cols
    width = 2 if members % 2 == 0 else 1
    me = {a: lax.axis_index(a) for a in axes}
    n = dict(zip(axes, sizes))

    def device(**at):
        return tuple(at.get(a, me[a]) for a in axes)

    def place(to):
        index = 0
        for size, at in zip(sizes, to):
            index = index * size + at
        return index

    lat, lon = me["lat"], me["lon"]
    left = lax.rem(lon + n["lon"] - 1, n["lon"])
    right = lax.rem(lon + 1, n["lon"])
    has_up = lat > 0
    has_down = lat < n["lat"] - 1
    steps = [s for s in itertools.product(*(range(size) for size in sizes)) if any(s)]

    def ahead(step):
        return tuple(lax.rem(me[a] + d, n[a]) if d else me[a] for a, d in zip(axes, step))

    deep = per * HALF
    head, tail = pl.ds(0, 3 * deep), pl.ds(3 * deep, rows - 3 * deep)
    front, back_rows = pl.ds(deep, deep), pl.ds(2 * deep, rows - 2 * deep)
    loads = [
        pltpu.make_async_copy(control.at[:, head], ext.at[:, pl.ds(HALF, 3 * deep)], local_sem.at[0]),
        pltpu.make_async_copy(vertical, vert, local_sem.at[1]),
        pltpu.make_async_copy(ensemble.at[:, front], ens.at[:, front], local_sem.at[2]),
        pltpu.make_async_copy(ensemble.at[:, back_rows], ens.at[:, back_rows], local_sem.at[3]),
        pltpu.make_async_copy(lat_taps, taps1, local_sem.at[4]),
        pltpu.make_async_copy(lon_taps, taps2, local_sem.at[5]),
        pltpu.make_async_copy(ensemble.at[:, pl.ds(0, deep)], ens.at[:, pl.ds(0, deep)], local_sem.at[6]),
        pltpu.make_async_copy(precision, prec, local_sem.at[7]),
        pltpu.make_async_copy(
            control.at[:, tail], ext.at[:, pl.ds(HALF + 3 * deep, rows - 3 * deep)], local_sem.at[8]
        ),
    ]
    for at in (4, 5, 0, 2, 1, 8, 3, 6, 7):
        loads[at].start()

    barrier = pltpu.get_barrier_semaphore()
    plane = [s for s in steps if not s[axes.index("lat")]]

    def signal(semaphore, to):
        pl.semaphore_signal(semaphore, inc=1, device_id=to, device_id_type=pl.DeviceIdType.MESH)

    for step in plane:
        signal(barrier, ahead(step))
    for has, row in ((has_up, lat - 1), (has_down, lat + 1)):
        @pl.when(has)
        def _():
            for col in (lon, left, right):
                signal(barrier, device(lat=row, lon=col))
    beside = jnp.where(has_up, 1, 0) + jnp.where(has_down, 1, 0)

    def hello(turn):
        for has, row in ((has_up, lat - 1), (has_down, lat + 1)):
            @pl.when(has)
            def _():
                signal(met.at[turn], device(lat=row))

    def hear(turn):
        pl.semaphore_wait(met.at[turn], beside)

    def remote(src, dst, send, recv, to):
        return pltpu.make_async_remote_copy(
            src_ref=src, dst_ref=dst, send_sem=send, recv_sem=recv,
            device_id=to, device_id_type=pl.DeviceIdType.MESH,
        )

    def row_copies(phase, up_src, down_src, dst):
        up = remote(
            up_src, dst.at[:, pl.ds(rows + HALF, HALF)],
            row_send.at[phase, 0], row_recv.at[phase, 0], device(lat=lat - 1),
        )
        down = remote(
            down_src, dst.at[:, pl.ds(0, HALF)],
            row_send.at[phase, 1], row_recv.at[phase, 1], device(lat=lat + 1),
        )
        return [up], [down]

    def corner_copies(phase, src, dst):
        up, down = [], []
        for side, to in ((0, left), (1, right)):
            there = dst.at[1 - side]
            mine = src.at[side]
            up.append(remote(
                mine.at[:, 0], there.at[:, groups + 1],
                corner_send.at[phase, 0], corner_recv.at[phase, 0], device(lat=lat - 1, lon=to),
            ))
            down.append(remote(
                mine.at[:, groups - 1], there.at[:, 0],
                corner_send.at[phase, 1], corner_recv.at[phase, 1], device(lat=lat + 1, lon=to),
            ))
        return up, down

    def corner_waits(phase, src, dst):
        up = remote(
            src.at[:, :, 0], dst.at[:, :, groups + 1],
            corner_send.at[phase, 0], corner_recv.at[phase, 0], device(lat=lat - 1, lon=left),
        )
        down = remote(
            src.at[:, :, groups - 1], dst.at[:, :, 0],
            corner_send.at[phase, 1], corner_recv.at[phase, 1], device(lat=lat + 1, lon=left),
        )
        return [up], [down]

    def piece(phase, k):
        if phase == 1:
            return k * per, per
        if k == 0:
            return 0, 1
        if k == chunks:
            return groups - per + 1, per - 1
        return (k - 1) * per + 1, per

    def side_copies(phase, src, dst, k):
        at, size = piece(phase, k)
        return [
            remote(
                src.at[side, :, pl.ds(at, size)], dst.at[1 - side, :, pl.ds(at + 1, size)],
                side_send.at[phase], side_recv.at[phase, k], device(lon=to),
            )
            for side, to in ((0, left), (1, right))
        ]

    def side_arrival(phase, src, dst, k):
        at, size = piece(phase, k)
        return remote(
            src.at[:, :, pl.ds(at, size)], dst.at[:, :, pl.ds(at + 1, size)],
            side_send.at[phase], side_recv.at[phase, k], device(lon=left),
        )

    def inc_copies(chunk, part):
        at = pl.ds(chunk * per, per)
        field = (inners, rims)[part].at[me["mem"], at]
        return [
            remote(
                field, field, inc_send.at[part, step - 1], inc_recv.at[part, step - 1, chunk],
                device(mem=lax.rem(me["mem"] + step, n["mem"])),
            )
            for step in range(1, n["mem"])
        ]

    def inc_arrivals(chunk, part):
        at = pl.ds(chunk * per, per)
        arrivals = []
        for step in range(1, n["mem"]):
            peer = lax.rem(me["mem"] + n["mem"] - step, n["mem"])
            field = (inners, rims)[part].at[peer, at]
            arrivals.append(remote(
                field, field, inc_send.at[part, step - 1], inc_recv.at[part, step - 1, chunk], device(mem=peer)
            ))
        return arrivals

    def each(has, copies, act):
        @pl.when(has)
        def _():
            for copy in copies:
                getattr(copy, act)()

    @pl.when(jnp.logical_not(has_up))
    def _():
        for one, two in ((ext, halo), (ext2, halo2)):
            one[:, 0:HALF] = jnp.zeros((members, HALF, cols, levels), BF16)
            for side in range(2):
                two[side, :, 0] = jnp.zeros((members, HALF * HALF, levels), BF16)

    @pl.when(jnp.logical_not(has_down))
    def _():
        for one, two in ((ext, halo), (ext2, halo2)):
            one[:, rows + HALF : rows + 2 * HALF] = jnp.zeros((members, HALF, cols, levels), BF16)
            for side in range(2):
                two[side, :, groups + 1] = jnp.zeros((members, HALF * HALF, levels), BF16)

    with jax.named_scope("taps"):
        loads[4].wait()
        loads[5].wait()
    with jax.named_scope("filt"):
        mid[...] = inner_matrix(taps1, taps2, cols, False)

    first = iota((2 * HALF, levels), 0) < HALF

    def edges(block):
        tile = 2 * HALF
        near = [block[cols * r : cols * r + tile] for r in range(HALF)]
        far = [block[cols * (r + 1) - tile : cols * (r + 1)] for r in range(HALF)]
        lefts = [jnp.where(first, near[r], pltpu.roll(near[r + 1], HALF, 0)) for r in range(0, HALF, 2)]
        rights = [jnp.where(first, pltpu.roll(far[r], HALF, 0), far[r + 1]) for r in range(0, HALF, 2)]
        return jnp.concatenate(lefts, axis=0).astype(BF16), jnp.concatenate(rights, axis=0).astype(BF16)

    def pack_group(go, carry):
        for m in range(members):
            block = ext[m, pl.ds(HALF * (go + 1), HALF)].reshape(cells, levels).astype(F32)
            stage[0, m, go], stage[1, m, go] = edges(block)
        return carry

    half = chunks // 2
    tile = 2 * HALF
    loads[1].wait()
    v = vert[...].astype(F32)
    vt = v.T
    blank = jnp.zeros((levels, levels), F32)

    def diagonal(block):
        if width == 1:
            return block.astype(BF16)
        return jnp.concatenate(
            [jnp.concatenate([block, blank], axis=1), jnp.concatenate([blank, block], axis=1)], axis=0
        ).astype(BF16)

    vert2[...] = diagonal(v)
    vert2t[...] = diagonal(vt)
    sums[...] = jnp.zeros_like(sums)

    def tile_sum(x):
        return jnp.sum(x.reshape(-1, 8, levels), axis=0)

    def squares(go, total):
        for m in range(members):
            block = ext[m, pl.ds(HALF * (go + 1), HALF)].reshape(cells, levels).astype(F32)
            total = total + tile_sum(block * block)
        return total

    def halves(matrix, data):
        both = dot(matrix[...], data)
        size = both.shape[0] // 2
        return both[:size] + both[size:]

    def smooth_inner(source, matrix, go, pair):
        data = [source[m, pl.ds(HALF * go, 3 * HALF)].reshape(3 * cells, levels) for m in pair]
        return halves(matrix, jnp.concatenate(data, axis=1))

    def smooth_rim(source, sides, matrices, go, pair):
        ends = []
        for side, matrix in enumerate(matrices):
            data = [
                jnp.concatenate([
                    source[m, pl.ds(HALF * go, 3 * HALF), (cols - 2 * tile) * side : (cols - 2 * tile) * side + 2 * tile]
                    .reshape(3 * HALF * 2 * tile, levels),
                    sides[side, m, pl.ds(go, 3)].reshape(3 * HALF * HALF, levels),
                ], axis=0)
                for m in pair
            ]
            ends.append(halves(matrix, jnp.concatenate(data, axis=1)))
        return jnp.concatenate(ends, axis=0)

    pairs = [tuple(range(m, m + width)) for m in range(0, members, width)]

    def inner_rows(x):
        return jnp.concatenate([x[cols * r + tile : cols * (r + 1) - tile] for r in range(HALF)], axis=0)

    def rim_rows(x):
        lefts = [x[cols * r : cols * r + tile] for r in range(HALF)]
        rights = [x[cols * (r + 1) - tile : cols * (r + 1)] for r in range(HALF)]
        return jnp.concatenate(lefts + rights, axis=0)

    def merge_rows(inner, rim):
        span = cols - 2 * tile
        blocks = []
        for r in range(HALF):
            blocks += [
                rim[tile * r : tile * (r + 1)], inner[span * r : span * (r + 1)],
                rim[tile * (HALF + r) : tile * (HALF + r + 1)],
            ]
        return jnp.concatenate(blocks, axis=0)

    def spread_of(m, go):
        return ens[m, pl.ds(HALF * go, HALF)].reshape(cells, levels).astype(F32)

    def contribute(places, smoothed, pick, field):
        leveled = dot(jnp.concatenate(smoothed, axis=0), vert2[...])
        size = leveled.shape[0] // len(smoothed)
        at = 0
        for go in places:
            total = None
            for pair in pairs:
                level = leveled[at : at + size]
                at += size
                for j, m in enumerate(pair):
                    term = pick(spread_of(m, go)) * level[:, j * levels : (j + 1) * levels]
                    total = term if total is None else total + term
            field[me["mem"], go] = total.astype(BF16)

    def places_of(chunk):
        return [chunk * per + g for g in range(per)]

    def forward_inner(chunk):
        places = places_of(chunk)
        smoothed = [smooth_inner(ext, mid, go, pair).astype(BF16) for go in places for pair in pairs]
        contribute(places, smoothed, inner_rows, inners)

    def forward_rim(some):
        places = [go for chunk in some for go in places_of(chunk)]
        smoothed = [smooth_rim(ext, halo, (near, far), go, pair).astype(BF16) for go in places for pair in pairs]
        contribute(places, smoothed, rim_rows, rims)

    def weigh(chunk):
        for g in range(per):
            go = chunk * per + g
            inner, rim = inners[0, go].astype(F32), rims[0, go].astype(F32)
            for peer in range(1, n["mem"]):
                inner = inner + inners[peer, go].astype(F32)
                rim = rim + rims[peer, go].astype(F32)
            increment = merge_rows(inner, rim)
            weighted = prec[pl.ds(HALF * go, HALF)].reshape(cells, levels) * increment
            sums[...] += tile_sum(weighted * increment)
            wgt[go] = weighted

    def adjoint(chunk):
        places = [chunk * per + g for g in range(per)]
        rows_of = []
        for go in places:
            weighted = wgt[go]
            for pair in pairs:
                parts_of = []
                for m in pair:
                    parts_of.append((spread_of(m, go) * weighted).astype(BF16))
                rows_of.append(jnp.concatenate(parts_of, axis=1))
        result = dot(jnp.concatenate(rows_of, axis=0), vert2t[...])
        at = 0
        for go in places:
            for pair in pairs:
                for j, m in enumerate(pair):
                    block = result[at : at + cells, j * levels : (j + 1) * levels]
                    ext2[m, pl.ds(HALF * (go + 1), HALF)] = block.astype(BF16).reshape(HALF, cols, levels)
                    stage2[0, m, go], stage2[1, m, go] = edges(block)
                at += cells
        for copy in side_copies(1, stage2, halo2, chunk):
            copy.start()

    def smooth(source, sides, matrix, go, pair):
        data = [
            jnp.concatenate([
                source[m, pl.ds(HALF * go, 3 * HALF)].reshape(3 * cells, levels),
                sides[0, m, pl.ds(go, 3)].reshape(3 * HALF * HALF, levels),
                sides[1, m, pl.ds(go, 3)].reshape(3 * HALF * HALF, levels),
            ], axis=0)
            for m in pair
        ]
        return halves(matrix, jnp.concatenate(data, axis=1))

    def final(chunk):
        for go in places_of(chunk):
            for pair in pairs:
                back = smooth(ext2, halo2, filt2, go, pair)
                for j, m in enumerate(pair):
                    held = ext[m, pl.ds(HALF * (go + 1), HALF)].astype(F32)
                    block = back[:, j * levels : (j + 1) * levels].reshape(HALF, cols, levels)
                    hess[m, pl.ds(HALF * go, HALF)] = held + block

    def wait_sides(phase, src, dst, chunk):
        side_arrival(phase, src, dst, chunk).wait_recv()

    row2_up, row2_down = row_copies(
        1, ext2.at[:, pl.ds(HALF, HALF)], ext2.at[:, pl.ds(rows, HALF)], ext2
    )
    corner2_up, corner2_down = corner_copies(1, stage2, halo2)
    both2_up, both2_down = corner_waits(1, stage2, halo2)

    across = [s for s in steps if not s[axes.index("mem")]]
    mine = lat * n["lon"] + lon
    part_out = [remote(parts.at[mine], parts.at[mine], part_sem.at[0], part_sem.at[1], ahead(step)) for step in across]
    others = parts.at[pl.ds(0, max(len(across), 1))]
    part_all = remote(others, others, part_sem.at[0], part_sem.at[1], ahead(steps[0]))
    norm = norms.at[me["mem"]]
    norm_out, norm_in = [], []
    for step in range(1, n["mem"]):
        to = lax.rem(me["mem"] + step, n["mem"])
        norm_out.append(remote(norm, norm, norm_send.at[step - 1], norm_recv.at[step - 1], device(mem=to)))
        of = lax.rem(me["mem"] + n["mem"] - step, n["mem"])
        norm_in.append(remote(norms.at[of], norms.at[of], norm_send.at[step - 1], norm_recv.at[step - 1], device(mem=of)))

    seen = {0: set(), 1: set()}

    def need_sides(phase, chunk):
        wanted = (chunk, chunk + 1) if phase == 0 else (chunk - 1, chunk, chunk + 1)
        for k in wanted:
            if 0 <= k < chunks + (phase == 0) and k not in seen[phase] and piece(phase, k)[1] > 0:
                seen[phase].add(k)
                wait_sides(phase, *((stage, halo) if phase == 0 else (stage2, halo2)), k)

    row_up, row_down = row_copies(
        0, ext.at[:, pl.ds(HALF, HALF)], ext.at[:, pl.ds(rows, HALF)], ext
    )
    corner_up, corner_down = corner_copies(0, stage, halo)
    both_up, both_down = corner_waits(0, stage, halo)

    def start_inc(chunk, part):
        for copy in inc_copies(chunk, part):
            copy.start()

    def do_inner(chunk):
        if chunk == 0:
            with jax.named_scope("rowwait"):
                each(has_up, row_down, "wait_recv")
        if chunk == chunks - 1:
            with jax.named_scope("rowwait"):
                each(has_down, row_up, "wait_recv")
        with jax.named_scope("inner"):
            forward_inner(chunk)

    def do_rim(*some):
        with jax.named_scope("rimwait"):
            for chunk in some:
                need_sides(0, chunk)
                if chunk == 0:
                    each(has_up, both_down, "wait_recv")
                if chunk == chunks - 1:
                    each(has_down, both_up, "wait_recv")
        with jax.named_scope("rim"):
            forward_rim(some)
            for chunk in some:
                start_inc(chunk, 1)

    adjointed = set()

    def do_adjoint(chunk):
        with jax.named_scope("incwait"):
            for part in range(2):
                for copy in inc_arrivals(chunk, part):
                    copy.wait_recv()
        with jax.named_scope("weigh"):
            weigh(chunk)
        adjointed.add(chunk)
        if len(adjointed) == chunks:
            with jax.named_scope("part"):
                for copy in norm_in:
                    copy.wait_recv()
                total = sums[...]
                for peer in range(n["mem"]):
                    total = total + norms[peer]
                parts[mine] = jnp.sum(total, axis=0, keepdims=True)
                for copy in part_out:
                    copy.start()
        with jax.named_scope("adj"):
            adjoint(chunk)
            if chunk == 0:
                each(has_up, row2_up + corner2_up, "start")
            if chunk == chunks - 1:
                each(has_down, row2_down + corner2_down, "start")

    def do_final(chunk):
        with jax.named_scope("bwait"):
            need_sides(1, chunk)
            if chunk == 0:
                each(has_up, row2_down + both2_down, "wait_recv")
            if chunk == chunks - 1:
                each(has_down, row2_up + both2_up, "wait_recv")
        with jax.named_scope("fin"):
            final(chunk)

    middle = list(range(1, chunks - 1))
    turns = n["lat"] - 1
    with jax.named_scope("load0"):
        loads[0].wait()
        loads[2].wait()
    do_inner(middle[0])
    with jax.named_scope("barrier"):
        pl.semaphore_wait(barrier, len(plane) + 3 * beside)
    start_inc(middle[0], 0)
    each(has_up, row_up, "start")
    with jax.named_scope("load8"):
        loads[8].wait()
    each(has_down, row_down, "start")
    with jax.named_scope("pack"):
        lax.fori_loop(0, groups, pack_group, 0, unroll=4)
    for k in [*range(1, half + 1), 0, chunks - 1, chunks, *range(half + 1, chunks - 1)]:
        if piece(0, k)[1] > 0:
            for copy in side_copies(0, stage, halo, k):
                copy.start()
        if k == 0:
            each(has_up, corner_up, "start")
            each(has_down, corner_down, "start")
    met_turns = []

    def meet():
        turn = len(met_turns)
        if turn > turns:
            return
        met_turns.append(turn)
        with jax.named_scope("meet"):
            if turn > 0:
                hear(turn - 1)
            if turn < turns:
                hello(turn)

    meet()
    with jax.named_scope("load3"):
        loads[3].wait()
        loads[6].wait()
    for chunk in middle[1:]:
        do_inner(chunk)
        start_inc(chunk, 0)
        if chunk == middle[half - 1]:
            meet()
    with jax.named_scope("filt1"):
        near[...] = rim_matrix(taps1, taps2, 0, False)
        far[...] = rim_matrix(taps1, taps2, 1, False)
    with jax.named_scope("load7"):
        loads[7].wait()
    last = chunks - 1
    lead = middle[: half - 1]
    rest = [c for c in middle if c not in lead and c != last - 1]
    order = [*lead, 0, last, *rest, last - 1]

    def do_end(chunk):
        do_inner(chunk)
        start_inc(chunk, 0)

    for chunk in lead:
        do_rim(chunk)
        if chunk == lead[-1]:
            meet()
    do_end(0)
    do_rim(0)
    do_end(last)
    with jax.named_scope("filt2"):
        filt2[...] = full_matrix(taps1, taps2, cols, True)
    do_rim(last)
    do_adjoint(order[0])
    if rest:
        do_rim(*rest)
    do_adjoint(order[1])
    do_rim(last - 1)
    with jax.named_scope("squares"):
        norms[me["mem"]] = lax.fori_loop(0, groups, squares, jnp.zeros((8, levels), F32), unroll=2)
        for copy in norm_out:
            copy.start()
    at = 2
    for position, now in enumerate(order):
        if position < at:
            continue
        if position == chunks - 2:
            while len(met_turns) <= turns:
                meet()
        do_adjoint(now)
    done = {c: max(order.index(d) for d in (c - 1, c, c + 1)) for c in middle}
    for chunk in sorted(middle, key=lambda c: (done[c], c)):
        do_final(chunk)
    do_final(last)
    do_final(0)

    with jax.named_scope("redend"):
        if across:
            part_all.wait_recv()
        curv[0, 0] = jnp.sum(parts[...]) * (1.0 / entries)

    with jax.named_scope("finish"):
        if across:
            part_all.wait_send()
        for copy in norm_out:
            copy.wait_send()
        each(has_up, row_up + both_up + row2_up + both2_up, "wait_send")
        each(has_down, row_down + both_down + row2_down + both2_down, "wait_send")
        for phase, src, dst in ((0, stage, halo), (1, stage2, halo2)):
            remote(src, dst.at[:, :, pl.ds(1, groups)], side_send.at[phase], side_recv.at[phase, 0], device(lon=left)).wait_send()
        for part, field in ((0, inners), (1, rims)):
            for step in range(1, n["mem"]):
                to = lax.rem(me["mem"] + step, n["mem"])
                whole = field.at[me["mem"]]
                remote(
                    whole, whole, inc_send.at[part, step - 1], inc_recv.at[part, step - 1, 0], device(mem=to)
                ).wait_send()


def per_device(axes, sizes, control, ensemble, precision, lat_taps, lon_taps, vertical):
    members, rows, cols, levels = control.shape
    n = dict(zip(axes, sizes))
    groups = rows // HALF
    cells = HALF * cols
    pack = HALF * HALF
    entries = control.size
    for size in sizes:
        entries *= size
    chunks = next(c for c in (8, 4, groups) if groups % c == 0)
    width = 2 if members % 2 == 0 else 1
    rim = 4 * pack
    smem = pl.BlockSpec(memory_space=pltpu.SMEM)
    anyspace = pl.BlockSpec(memory_space=pltpu.HBM)
    peers = max(n["mem"] - 1, 1)
    hessian, curvature = pl.pallas_call(
        functools.partial(kernel, axes, sizes, entries, chunks),
        out_shape=(
            pltpu.VMEM(control.shape, F32),
            jax.ShapeDtypeStruct((1, 1), F32),
        ),
        in_specs=[anyspace, anyspace, anyspace, anyspace, anyspace, anyspace],
        out_specs=(pl.BlockSpec(memory_space=pltpu.VMEM), smem),
        scratch_shapes=[
            pltpu.VMEM((members, rows + 2 * HALF, cols, levels), BF16),
            pltpu.VMEM((members, rows + 2 * HALF, cols, levels), BF16),
            pltpu.VMEM(control.shape, BF16),
            pltpu.VMEM(precision.shape, F32),
            pltpu.VMEM((groups, cells, levels), F32),
            pltpu.VMEM((n["mem"], groups, cells - rim, levels), BF16),
            pltpu.VMEM((n["mem"], groups, rim, levels), BF16),
            pltpu.VMEM((2, members, groups + 2, pack, levels), BF16),
            pltpu.VMEM((2, members, groups + 2, pack, levels), BF16),
            pltpu.VMEM((2, members, groups, pack, levels), BF16),
            pltpu.VMEM((2, members, groups, pack, levels), BF16),
            pltpu.VMEM((2 * (cells - rim), 3 * cells), BF16),
            pltpu.VMEM((rim, 15 * pack), BF16),
            pltpu.VMEM((rim, 15 * pack), BF16),
            pltpu.VMEM((2 * cells, 3 * cells + 6 * pack), BF16),
            pltpu.VMEM((levels, levels), BF16),
            pltpu.VMEM((width * levels, width * levels), BF16),
            pltpu.VMEM((width * levels, width * levels), BF16),
            pltpu.VMEM((8, levels), F32),
            pltpu.VMEM((n["lat"] * n["lon"], 1, levels), F32),
            pltpu.VMEM((n["mem"], 8, levels), F32),
            pltpu.SMEM(lat_taps.shape, F32),
            pltpu.SMEM(lon_taps.shape, F32),
            pltpu.SemaphoreType.DMA((9,)),
            pltpu.SemaphoreType.DMA((2, 2)),
            pltpu.SemaphoreType.DMA((2, 2)),
            pltpu.SemaphoreType.DMA((2, 2)),
            pltpu.SemaphoreType.DMA((2, 2)),
            pltpu.SemaphoreType.DMA((2,)),
            pltpu.SemaphoreType.DMA((2, chunks + 1)),
            pltpu.SemaphoreType.DMA((2, peers)),
            pltpu.SemaphoreType.DMA((2, peers, chunks)),
            pltpu.SemaphoreType.DMA((2,)),
            pltpu.SemaphoreType.DMA((peers,)),
            pltpu.SemaphoreType.DMA((peers,)),
            pltpu.SemaphoreType.REGULAR((max(n["lat"] - 1, 1),)),
        ],
        compiler_params=pltpu.CompilerParams(
            collective_id=0, has_side_effects=True, vmem_limit_bytes=59 * 1024 * 1024
        ),
    )(lat_taps, lon_taps, control, ensemble, precision, vertical)
    return hessian, curvature.reshape(())


def solution(mesh):
    axes = tuple(mesh.axis_names)
    sizes = tuple(mesh.shape[a] for a in axes)
    in_specs = (
        P("mem", "lat", "lon", None),
        P("mem", "lat", "lon", None),
        P("lat", "lon", None),
        P(),
        P(),
        P(),
    )
    out_specs = (P("mem", "lat", "lon", None), P())
    return jax.shard_map(
        functools.partial(per_device, axes, sizes),
        mesh=mesh, in_specs=in_specs, out_specs=out_specs, check_vma=False,
    )
```

```python
import functools
import itertools

import jax
import jax.numpy as jnp
from jax import lax
from jax.experimental import pallas as pl
from jax.experimental.pallas import tpu as pltpu
from jax.sharding import PartitionSpec as P

F32 = jnp.float32
BF16 = jnp.bfloat16
HALF = 4


def iota(shape, dim):
    return lax.broadcasted_iota(jnp.int32, shape, dim)


def tap_products(lat_taps, lon_taps, down, across, reverse):
    taps = lat_taps.shape[0]
    first = jnp.zeros(down.shape, F32)
    second = jnp.zeros(down.shape, F32)
    for tap in range(taps):
        at = taps - 1 - tap if reverse else tap
        first = jnp.where(down == tap, lat_taps[at], first)
        second = jnp.where(across == tap, lon_taps[at], second)
    full = first * second
    high = full.astype(BF16)
    low = (full - high.astype(F32)).astype(BF16)
    return jnp.concatenate([high, low], axis=0)


def full_matrix(lat_taps, lon_taps, cols, reverse):
    shape = (HALF * cols, 3 * HALF * cols + 6 * HALF * HALF)
    out, src = iota(shape, 0), iota(shape, 1)
    main = 3 * HALF * cols
    side = 3 * HALF * HALF
    inside = src < main
    left = src < main + side
    packed = jnp.where(left, src - main, src - main - side)
    row = jnp.where(inside, src // cols, packed // HALF)
    col = jnp.where(
        inside, src % cols, packed % HALF + jnp.where(left, -HALF, cols)
    )
    return tap_products(lat_taps, lon_taps, row - out // cols, col - out % cols + HALF, reverse)


def inner_matrix(lat_taps, lon_taps, cols, reverse):
    span = cols - 4 * HALF
    shape = (HALF * span, 3 * HALF * cols)
    out, src = iota(shape, 0), iota(shape, 1)
    down = src // cols - out // span
    across = src % cols - (out % span + 2 * HALF) + HALF
    return tap_products(lat_taps, lon_taps, down, across, reverse)


def rim_matrix(lat_taps, lon_taps, side, reverse):
    tile = 2 * HALF
    main = 3 * HALF * 2 * tile
    shape = (HALF * tile, main + 3 * HALF * HALF)
    out, src = iota(shape, 0), iota(shape, 1)
    inside = src < main
    packed = src - main
    row = jnp.where(inside, src // (2 * tile), packed // HALF)
    col = jnp.where(inside, src % (2 * tile), packed % HALF + (2 * tile if side else -HALF))
    down = row - out // tile
    across = col - (out % tile + (tile if side else 0)) + HALF
    return tap_products(lat_taps, lon_taps, down, across, reverse)


def dot(a, b):
    return jnp.dot(a, b, preferred_element_type=F32)


def kernel(
    axes, sizes, entries, chunks, lat_taps, lon_taps, control, ensemble, precision, vertical, hess, curv,
    ext, ext2, ens, prec, wgt, inners, rims, halo, halo2, stage, stage2,
    mid, near, far, filt2, vert, vert2, vert2t, sums, parts, norms, taps1, taps2,
    local_sem, row_send, row_recv, corner_send, corner_recv, side_send, side_recv, inc_send, inc_recv, part_sem, norm_send, norm_recv, met,
):
    members, rows, cols, levels = control.shape
    groups = rows // HALF
    per = groups // chunks
    cells = HALF * cols
    width = 2 if members % 2 == 0 else 1
    me = {a: lax.axis_index(a) for a in axes}
    n = dict(zip(axes, sizes))

    def device(**at):
        return tuple(at.get(a, me[a]) for a in axes)

    def place(to):
        index = 0
        for size, at in zip(sizes, to):
            index = index * size + at
        return index

    lat, lon = me["lat"], me["lon"]
    left = lax.rem(lon + n["lon"] - 1, n["lon"])
    right = lax.rem(lon + 1, n["lon"])
    has_up = lat > 0
    has_down = lat < n["lat"] - 1
    steps = [s for s in itertools.product(*(range(size) for size in sizes)) if any(s)]

    def ahead(step):
        return tuple(lax.rem(me[a] + d, n[a]) if d else me[a] for a, d in zip(axes, step))

    deep = per * HALF
    first_rows = 2 * deep + HALF
    head, tail = pl.ds(0, first_rows), pl.ds(first_rows, rows - first_rows)
    front, back_rows = pl.ds(deep, deep), pl.ds(2 * deep, rows - 2 * deep)
    loads = [
        pltpu.make_async_copy(control.at[:, head], ext.at[:, pl.ds(HALF, first_rows)], local_sem.at[0]),
        pltpu.make_async_copy(vertical, vert, local_sem.at[1]),
        pltpu.make_async_copy(ensemble.at[:, front], ens.at[:, front], local_sem.at[2]),
        pltpu.make_async_copy(ensemble.at[:, back_rows], ens.at[:, back_rows], local_sem.at[3]),
        pltpu.make_async_copy(lat_taps, taps1, local_sem.at[4]),
        pltpu.make_async_copy(lon_taps, taps2, local_sem.at[5]),
        pltpu.make_async_copy(ensemble.at[:, pl.ds(0, deep)], ens.at[:, pl.ds(0, deep)], local_sem.at[6]),
        pltpu.make_async_copy(precision, prec, local_sem.at[7]),
        pltpu.make_async_copy(
            control.at[:, tail], ext.at[:, pl.ds(HALF + first_rows, rows - first_rows)], local_sem.at[8]
        ),
    ]
    for at in (4, 5, 1, 0, 2, 8, 3, 6, 7):
        loads[at].start()

    barrier = pltpu.get_barrier_semaphore()
    plane = [s for s in steps if not s[axes.index("lat")]]

    def signal(semaphore, to):
        pl.semaphore_signal(semaphore, inc=1, device_id=to, device_id_type=pl.DeviceIdType.MESH)

    for step in plane:
        signal(barrier, ahead(step))
    for has, row in ((has_up, lat - 1), (has_down, lat + 1)):
        @pl.when(has)
        def _():
            for col in (lon, left, right):
                signal(barrier, device(lat=row, lon=col))
    beside = jnp.where(has_up, 1, 0) + jnp.where(has_down, 1, 0)

    def hello(turn):
        for has, row in ((has_up, lat - 1), (has_down, lat + 1)):
            @pl.when(has)
            def _():
                signal(met.at[turn], device(lat=row))

    def hear(turn):
        pl.semaphore_wait(met.at[turn], beside)

    def remote(src, dst, send, recv, to):
        return pltpu.make_async_remote_copy(
            src_ref=src, dst_ref=dst, send_sem=send, recv_sem=recv,
            device_id=to, device_id_type=pl.DeviceIdType.MESH,
        )

    def row_copies(phase, up_src, down_src, dst):
        up = remote(
            up_src, dst.at[:, pl.ds(rows + HALF, HALF)],
            row_send.at[phase, 0], row_recv.at[phase, 0], device(lat=lat - 1),
        )
        down = remote(
            down_src, dst.at[:, pl.ds(0, HALF)],
            row_send.at[phase, 1], row_recv.at[phase, 1], device(lat=lat + 1),
        )
        return [up], [down]

    def corner_copies(phase, src, dst):
        up, down = [], []
        for side, to in ((0, left), (1, right)):
            there = dst.at[1 - side]
            mine = src.at[side]
            up.append(remote(
                mine.at[:, 0], there.at[:, groups + 1],
                corner_send.at[phase, 0], corner_recv.at[phase, 0], device(lat=lat - 1, lon=to),
            ))
            down.append(remote(
                mine.at[:, groups - 1], there.at[:, 0],
                corner_send.at[phase, 1], corner_recv.at[phase, 1], device(lat=lat + 1, lon=to),
            ))
        return up, down

    def corner_waits(phase, src, dst):
        up = remote(
            src.at[:, :, 0], dst.at[:, :, groups + 1],
            corner_send.at[phase, 0], corner_recv.at[phase, 0], device(lat=lat - 1, lon=left),
        )
        down = remote(
            src.at[:, :, groups - 1], dst.at[:, :, 0],
            corner_send.at[phase, 1], corner_recv.at[phase, 1], device(lat=lat + 1, lon=left),
        )
        return [up], [down]

    half = chunks // 2
    sets = [[1, 2], *[[k] for k in range(3, half + 1)], [0], [chunks - 1, chunks], list(range(half + 1, chunks - 1))]
    sets = [ks for ks in sets if ks]

    def piece(phase, k):
        if phase == 1:
            return k * per, per
        ks = sets[k]
        start = max((ks[0] - 1) * per + 1, 0)
        return start, min(ks[-1] * per + 1, groups) - start

    def side_sem(phase, k):
        return side_recv.at[phase * len(sets) + k]

    def side_copies(phase, src, dst, k):
        at, size = piece(phase, k)
        return [
            remote(
                src.at[side, :, pl.ds(at, size)], dst.at[1 - side, :, pl.ds(at + 1, size)],
                side_send.at[phase], side_sem(phase, k), device(lon=to),
            )
            for side, to in ((0, left), (1, right))
        ]

    def side_arrival(phase, src, dst, k):
        at, size = piece(phase, k)
        return remote(
            src.at[:, :, pl.ds(at, size)], dst.at[:, :, pl.ds(at + 1, size)],
            side_send.at[phase], side_sem(phase, k), device(lon=left),
        )

    def inc_sem(chunk, part):
        return chunk if part else chunks + (chunk == 0) + 2 * (chunk == chunks - 1)

    def inc_copies(chunk, part):
        at = pl.ds(chunk * per, per)
        field = (inners, rims)[part].at[me["mem"], at]
        return [
            remote(
                field, field, inc_send.at[part, step - 1], inc_recv.at[step - 1, inc_sem(chunk, part)],
                device(mem=lax.rem(me["mem"] + step, n["mem"])),
            )
            for step in range(1, n["mem"])
        ]

    def inc_arrivals(chunk, part):
        first, count = chunk, 1
        if part == 0 and 0 < chunk < chunks - 1:
            if "inner" in arrived:
                return []
            arrived.add("inner")
            first, count = 1, chunks - 2
        at = pl.ds(first * per, count * per)
        arrivals = []
        for step in range(1, n["mem"]):
            peer = lax.rem(me["mem"] + n["mem"] - step, n["mem"])
            field = (inners, rims)[part].at[peer, at]
            arrivals.append(remote(
                field, field, inc_send.at[part, step - 1], inc_recv.at[step - 1, inc_sem(chunk, part)], device(mem=peer)
            ))
        return arrivals

    arrived = set()

    def each(has, copies, act):
        @pl.when(has)
        def _():
            for copy in copies:
                getattr(copy, act)()

    @pl.when(jnp.logical_not(has_up))
    def _():
        for one, two in ((ext, halo), (ext2, halo2)):
            one[:, 0:HALF] = jnp.zeros((members, HALF, cols, levels), BF16)
            for side in range(2):
                two[side, :, 0] = jnp.zeros((members, HALF * HALF, levels), BF16)

    @pl.when(jnp.logical_not(has_down))
    def _():
        for one, two in ((ext, halo), (ext2, halo2)):
            one[:, rows + HALF : rows + 2 * HALF] = jnp.zeros((members, HALF, cols, levels), BF16)
            for side in range(2):
                two[side, :, groups + 1] = jnp.zeros((members, HALF * HALF, levels), BF16)

    with jax.named_scope("taps"):
        loads[4].wait()
        loads[5].wait()
    with jax.named_scope("filt"):
        mid[...] = inner_matrix(taps1, taps2, cols, False)

    first = iota((2 * HALF, levels), 0) < HALF

    def edges(block):
        tile = 2 * HALF
        near = [block[cols * r : cols * r + tile] for r in range(HALF)]
        far = [block[cols * (r + 1) - tile : cols * (r + 1)] for r in range(HALF)]
        lefts = [jnp.where(first, near[r], pltpu.roll(near[r + 1], HALF, 0)) for r in range(0, HALF, 2)]
        rights = [jnp.where(first, pltpu.roll(far[r], HALF, 0), far[r + 1]) for r in range(0, HALF, 2)]
        return jnp.concatenate(lefts, axis=0).astype(BF16), jnp.concatenate(rights, axis=0).astype(BF16)

    def pack_group(go, carry):
        for m in range(members):
            block = ext[m, pl.ds(HALF * (go + 1), HALF)].reshape(cells, levels).astype(F32)
            stage[0, m, go], stage[1, m, go] = edges(block)
        return carry

    tile = 2 * HALF
    loads[1].wait()
    v = vert[...].astype(F32)
    vt = v.T
    blank = jnp.zeros((levels, levels), F32)

    def diagonal(block):
        if width == 1:
            return block.astype(BF16)
        return jnp.concatenate(
            [jnp.concatenate([block, blank], axis=1), jnp.concatenate([blank, block], axis=1)], axis=0
        ).astype(BF16)

    vert2[...] = diagonal(v)
    vert2t[...] = diagonal(vt)
    sums[...] = jnp.zeros_like(sums)

    def tile_sum(x):
        return jnp.sum(x.reshape(-1, 8, levels), axis=0)

    def squares(go, total):
        for m in range(members):
            block = ext[m, pl.ds(HALF * (go + 1), HALF)].reshape(cells, levels).astype(F32)
            total = total + tile_sum(block * block)
        return total

    def halves(matrix, data):
        both = dot(matrix[...], data)
        size = both.shape[0] // 2
        return both[:size] + both[size:]

    def smooth_inner(source, matrix, go, pair):
        data = [source[m, pl.ds(HALF * go, 3 * HALF)].reshape(3 * cells, levels) for m in pair]
        return halves(matrix, jnp.concatenate(data, axis=1))

    def smooth_rim(source, sides, matrices, go, pair):
        ends = []
        for side, matrix in enumerate(matrices):
            data = [
                jnp.concatenate([
                    source[m, pl.ds(HALF * go, 3 * HALF), (cols - 2 * tile) * side : (cols - 2 * tile) * side + 2 * tile]
                    .reshape(3 * HALF * 2 * tile, levels),
                    sides[side, m, pl.ds(go, 3)].reshape(3 * HALF * HALF, levels),
                ], axis=0)
                for m in pair
            ]
            ends.append(halves(matrix, jnp.concatenate(data, axis=1)))
        return jnp.concatenate(ends, axis=0)

    pairs = [tuple(range(m, m + width)) for m in range(0, members, width)]

    def inner_rows(x):
        return jnp.concatenate([x[cols * r + tile : cols * (r + 1) - tile] for r in range(HALF)], axis=0)

    def rim_rows(x):
        lefts = [x[cols * r : cols * r + tile] for r in range(HALF)]
        rights = [x[cols * (r + 1) - tile : cols * (r + 1)] for r in range(HALF)]
        return jnp.concatenate(lefts + rights, axis=0)

    def merge_rows(inner, rim):
        span = cols - 2 * tile
        blocks = []
        for r in range(HALF):
            blocks += [
                rim[tile * r : tile * (r + 1)], inner[span * r : span * (r + 1)],
                rim[tile * (HALF + r) : tile * (HALF + r + 1)],
            ]
        return jnp.concatenate(blocks, axis=0)

    def spread_of(m, go):
        return ens[m, pl.ds(HALF * go, HALF)].reshape(cells, levels).astype(F32)

    def contribute(places, smoothed, pick, field):
        leveled = dot(jnp.concatenate(smoothed, axis=0), vert2[...])
        size = leveled.shape[0] // len(smoothed)
        at = 0
        for go in places:
            total = None
            for pair in pairs:
                level = leveled[at : at + size]
                at += size
                for j, m in enumerate(pair):
                    term = pick(spread_of(m, go)) * level[:, j * levels : (j + 1) * levels]
                    total = term if total is None else total + term
            field[me["mem"], go] = total.astype(BF16)

    def places_of(chunk):
        return [chunk * per + g for g in range(per)]

    def forward_inner(chunk):
        places = places_of(chunk)
        smoothed = [smooth_inner(ext, mid, go, pair).astype(BF16) for go in places for pair in pairs]
        contribute(places, smoothed, inner_rows, inners)

    def forward_rim(some):
        places = [go for chunk in some for go in places_of(chunk)]
        smoothed = [smooth_rim(ext, halo, (near, far), go, pair).astype(BF16) for go in places for pair in pairs]
        contribute(places, smoothed, rim_rows, rims)

    def weigh(chunk):
        for g in range(per):
            go = chunk * per + g
            inner, rim = inners[0, go].astype(F32), rims[0, go].astype(F32)
            for peer in range(1, n["mem"]):
                inner = inner + inners[peer, go].astype(F32)
                rim = rim + rims[peer, go].astype(F32)
            increment = merge_rows(inner, rim)
            weighted = prec[pl.ds(HALF * go, HALF)].reshape(cells, levels) * increment
            sums[...] += tile_sum(weighted * increment)
            wgt[go] = weighted

    def adjoint(chunk):
        places = [chunk * per + g for g in range(per)]
        rows_of = []
        for go in places:
            weighted = wgt[go]
            for pair in pairs:
                parts_of = []
                for m in pair:
                    parts_of.append((spread_of(m, go) * weighted).astype(BF16))
                rows_of.append(jnp.concatenate(parts_of, axis=1))
        result = dot(jnp.concatenate(rows_of, axis=0), vert2t[...])
        at = 0
        for go in places:
            for pair in pairs:
                for j, m in enumerate(pair):
                    block = result[at : at + cells, j * levels : (j + 1) * levels]
                    ext2[m, pl.ds(HALF * (go + 1), HALF)] = block.astype(BF16).reshape(HALF, cols, levels)
                    stage2[0, m, go], stage2[1, m, go] = edges(block)
                at += cells
        for copy in side_copies(1, stage2, halo2, chunk):
            copy.start()

    def smooth(source, sides, matrix, go, pair):
        data = [
            jnp.concatenate([
                source[m, pl.ds(HALF * go, 3 * HALF)].reshape(3 * cells, levels),
                sides[0, m, pl.ds(go, 3)].reshape(3 * HALF * HALF, levels),
                sides[1, m, pl.ds(go, 3)].reshape(3 * HALF * HALF, levels),
            ], axis=0)
            for m in pair
        ]
        return halves(matrix, jnp.concatenate(data, axis=1))

    def final(chunk):
        for go in places_of(chunk):
            for pair in pairs:
                back = smooth(ext2, halo2, filt2, go, pair)
                for j, m in enumerate(pair):
                    held = ext[m, pl.ds(HALF * (go + 1), HALF)].astype(F32)
                    block = back[:, j * levels : (j + 1) * levels].reshape(HALF, cols, levels)
                    hess[m, pl.ds(HALF * go, HALF)] = held + block

    def wait_sides(phase, src, dst, chunk):
        side_arrival(phase, src, dst, chunk).wait_recv()

    row2_up, row2_down = row_copies(
        1, ext2.at[:, pl.ds(HALF, HALF)], ext2.at[:, pl.ds(rows, HALF)], ext2
    )
    corner2_up, corner2_down = corner_copies(1, stage2, halo2)
    both2_up, both2_down = corner_waits(1, stage2, halo2)

    across = [s for s in steps if not s[axes.index("mem")]]
    mine = lat * n["lon"] + lon
    part_out = [remote(parts.at[mine], parts.at[mine], part_sem.at[0], part_sem.at[1], ahead(step)) for step in across]
    others = parts.at[pl.ds(0, max(len(across), 1))]
    part_all = remote(others, others, part_sem.at[0], part_sem.at[1], ahead(steps[0]))
    norm = norms.at[me["mem"]]
    norm_out, norm_in = [], []
    for step in range(1, n["mem"]):
        to = lax.rem(me["mem"] + step, n["mem"])
        norm_out.append(remote(norm, norm, norm_send.at[step - 1], norm_recv.at[step - 1], device(mem=to)))
        of = lax.rem(me["mem"] + n["mem"] - step, n["mem"])
        norm_in.append(remote(norms.at[of], norms.at[of], norm_send.at[step - 1], norm_recv.at[step - 1], device(mem=of)))

    seen = {0: set(), 1: set()}

    def need_sides(phase, chunk):
        wanted = (chunk - 1, chunk, chunk + 1)
        if phase == 0:
            wanted = [i for i, ks in enumerate(sets) if chunk in ks or chunk + 1 in ks]
        for k in wanted:
            if 0 <= k < max(chunks, len(sets)) and k not in seen[phase] and piece(phase, k)[1] > 0:
                if phase == 1 and k >= chunks:
                    continue
                seen[phase].add(k)
                wait_sides(phase, *((stage, halo) if phase == 0 else (stage2, halo2)), k)

    row_up, row_down = row_copies(
        0, ext.at[:, pl.ds(HALF, HALF)], ext.at[:, pl.ds(rows, HALF)], ext
    )
    corner_up, corner_down = corner_copies(0, stage, halo)
    both_up, both_down = corner_waits(0, stage, halo)

    def start_inc(chunk, part):
        for copy in inc_copies(chunk, part):
            copy.start()

    def do_inner(chunk):
        if chunk == 0:
            with jax.named_scope("rowwait"):
                each(has_up, row_down, "wait_recv")
        if chunk == chunks - 1:
            with jax.named_scope("rowwait"):
                each(has_down, row_up, "wait_recv")
        with jax.named_scope("inner"):
            forward_inner(chunk)

    def do_rim(*some):
        with jax.named_scope("rimwait"):
            for chunk in some:
                need_sides(0, chunk)
                if chunk == 0:
                    each(has_up, both_down, "wait_recv")
                if chunk == chunks - 1:
                    each(has_down, both_up, "wait_recv")
        with jax.named_scope("rim"):
            forward_rim(some)
            for chunk in some:
                start_inc(chunk, 1)

    adjointed = set()

    def do_adjoint(chunk):
        with jax.named_scope("incwait"):
            for part in range(2):
                for copy in inc_arrivals(chunk, part):
                    copy.wait_recv()
        with jax.named_scope("weigh"):
            weigh(chunk)
        adjointed.add(chunk)
        if len(adjointed) == chunks:
            with jax.named_scope("part"):
                for copy in norm_in:
                    copy.wait_recv()
                total = sums[...]
                for peer in range(n["mem"]):
                    total = total + norms[peer]
                parts[mine] = jnp.sum(total, axis=0, keepdims=True)
                for copy in part_out:
                    copy.start()
        with jax.named_scope("adj"):
            adjoint(chunk)
            if chunk == 0:
                each(has_up, row2_up + corner2_up, "start")
            if chunk == chunks - 1:
                each(has_down, row2_down + corner2_down, "start")

    def do_final(chunk):
        with jax.named_scope("bwait"):
            need_sides(1, chunk)
            if chunk == 0:
                each(has_up, row2_down + both2_down, "wait_recv")
            if chunk == chunks - 1:
                each(has_down, row2_up + both2_up, "wait_recv")
        with jax.named_scope("fin"):
            final(chunk)

    middle = list(range(1, chunks - 1))
    turns = n["lat"] - 1
    with jax.named_scope("load0"):
        loads[0].wait()
        loads[2].wait()
    do_inner(middle[0])
    with jax.named_scope("barrier"):
        pl.semaphore_wait(barrier, len(plane) + 3 * beside)
    start_inc(middle[0], 0)
    with jax.named_scope("load8"):
        loads[8].wait()
    with jax.named_scope("pack"):
        lax.fori_loop(0, groups, pack_group, 0, unroll=4)
    waves = list(range(len(sets)))

    def send_sides():
        if not waves:
            return
        k = waves.pop(0)
        if piece(0, k)[1] > 0:
            for copy in side_copies(0, stage, halo, k):
                copy.start()
        if sets[k] == [0]:
            each(has_up, corner_up, "start")
            each(has_down, corner_down, "start")

    send_sides()
    each(has_up, row_up, "start")
    each(has_down, row_down, "start")
    while waves:
        send_sides()
    met_turns = []

    def meet():
        turn = len(met_turns)
        if turn > turns:
            return
        met_turns.append(turn)
        with jax.named_scope("meet"):
            if turn > 0:
                hear(turn - 1)
            if turn < turns:
                hello(turn)

    meet()
    with jax.named_scope("load3"):
        loads[3].wait()
        loads[6].wait()
    for chunk in middle[1:]:
        do_inner(chunk)
        start_inc(chunk, 0)
        send_sides()
        if chunk == middle[half - 1]:
            meet()
    while waves:
        send_sides()
    with jax.named_scope("filt1"):
        near[...] = rim_matrix(taps1, taps2, 0, False)
        far[...] = rim_matrix(taps1, taps2, 1, False)
    with jax.named_scope("squares"):
        norms[me["mem"]] = lax.fori_loop(0, groups, squares, jnp.zeros((8, levels), F32), unroll=2)
        for copy in norm_out:
            copy.start()
    with jax.named_scope("load7"):
        loads[7].wait()
    last = chunks - 1
    lead = middle[: half - 1]
    rest = [c for c in middle if c not in lead and c != last - 1]
    order = [*lead, 0, last, *rest, last - 1]

    def do_end(chunk):
        do_inner(chunk)
        start_inc(chunk, 0)

    for chunk in lead:
        do_rim(chunk)
        if chunk == lead[-1]:
            meet()
    do_end(0)
    do_rim(0)
    do_end(last)
    do_rim(last)
    ahead_of = half - 1
    do_adjoint(order[0])
    if rest:
        do_rim(*rest)
    do_adjoint(order[1])
    do_rim(last - 1)
    do_adjoint(order[2])
    do_adjoint(order[3])
    do_adjoint(order[4])
    with jax.named_scope("filt2"):
        filt2[...] = full_matrix(taps1, taps2, cols, True)
    while len(met_turns) <= turns:
        meet()
    done = {c: max(order.index(d) for d in (c - 1, c, c + 1)) for c in middle}
    finals = sorted(middle, key=lambda c: (done[c], c))
    slots = ()
    for now in order[ahead_of + 2 :]:
        do_adjoint(now)
        if order.index(now) in slots:
            do_final(finals.pop(0))
    for chunk in finals:
        do_final(chunk)
    do_final(last)
    do_final(0)

    with jax.named_scope("redend"):
        if across:
            part_all.wait_recv()
        curv[0, 0] = jnp.sum(parts[...]) * (1.0 / entries)

    with jax.named_scope("finish"):
        if across:
            part_all.wait_send()
        for copy in norm_out:
            copy.wait_send()
        each(has_up, row_up + both_up + row2_up + both2_up, "wait_send")
        each(has_down, row_down + both_down + row2_down + both2_down, "wait_send")
        for phase, src, dst in ((0, stage, halo), (1, stage2, halo2)):
            remote(src, dst.at[:, :, pl.ds(1, groups)], side_send.at[phase], side_recv.at[0], device(lon=left)).wait_send()
        for part, field in ((0, inners), (1, rims)):
            for step in range(1, n["mem"]):
                to = lax.rem(me["mem"] + step, n["mem"])
                whole = field.at[me["mem"]]
                remote(
                    whole, whole, inc_send.at[part, step - 1], inc_recv.at[step - 1, 0], device(mem=to)
                ).wait_send()


def per_device(axes, sizes, control, ensemble, precision, lat_taps, lon_taps, vertical):
    members, rows, cols, levels = control.shape
    n = dict(zip(axes, sizes))
    groups = rows // HALF
    cells = HALF * cols
    pack = HALF * HALF
    entries = control.size
    for size in sizes:
        entries *= size
    chunks = next(c for c in (8, 4, groups) if groups % c == 0)
    width = 2 if members % 2 == 0 else 1
    rim = 4 * pack
    smem = pl.BlockSpec(memory_space=pltpu.SMEM)
    anyspace = pl.BlockSpec(memory_space=pltpu.HBM)
    peers = max(n["mem"] - 1, 1)
    hessian, curvature = pl.pallas_call(
        functools.partial(kernel, axes, sizes, entries, chunks),
        out_shape=(
            pltpu.VMEM(control.shape, F32),
            jax.ShapeDtypeStruct((1, 1), F32),
        ),
        in_specs=[anyspace, anyspace, anyspace, anyspace, anyspace, anyspace],
        out_specs=(pl.BlockSpec(memory_space=pltpu.VMEM), smem),
        scratch_shapes=[
            pltpu.VMEM((members, rows + 2 * HALF, cols, levels), BF16),
            pltpu.VMEM((members, rows + 2 * HALF, cols, levels), BF16),
            pltpu.VMEM(control.shape, BF16),
            pltpu.VMEM(precision.shape, F32),
            pltpu.VMEM((groups, cells, levels), F32),
            pltpu.VMEM((n["mem"], groups, cells - rim, levels), BF16),
            pltpu.VMEM((n["mem"], groups, rim, levels), BF16),
            pltpu.VMEM((2, members, groups + 2, pack, levels), BF16),
            pltpu.VMEM((2, members, groups + 2, pack, levels), BF16),
            pltpu.VMEM((2, members, groups, pack, levels), BF16),
            pltpu.VMEM((2, members, groups, pack, levels), BF16),
            pltpu.VMEM((2 * (cells - rim), 3 * cells), BF16),
            pltpu.VMEM((rim, 15 * pack), BF16),
            pltpu.VMEM((rim, 15 * pack), BF16),
            pltpu.VMEM((2 * cells, 3 * cells + 6 * pack), BF16),
            pltpu.VMEM((levels, levels), BF16),
            pltpu.VMEM((width * levels, width * levels), BF16),
            pltpu.VMEM((width * levels, width * levels), BF16),
            pltpu.VMEM((8, levels), F32),
            pltpu.VMEM((n["lat"] * n["lon"], 1, levels), F32),
            pltpu.VMEM((n["mem"], 8, levels), F32),
            pltpu.SMEM(lat_taps.shape, F32),
            pltpu.SMEM(lon_taps.shape, F32),
            pltpu.SemaphoreType.DMA((9,)),
            pltpu.SemaphoreType.DMA((2, 2)),
            pltpu.SemaphoreType.DMA((2, 2)),
            pltpu.SemaphoreType.DMA((2, 2)),
            pltpu.SemaphoreType.DMA((2, 2)),
            pltpu.SemaphoreType.DMA((2,)),
            pltpu.SemaphoreType.DMA((chunks // 2 + chunks + 2,)),
            pltpu.SemaphoreType.DMA((2, peers)),
            pltpu.SemaphoreType.DMA((peers, chunks + 3)),
            pltpu.SemaphoreType.DMA((2,)),
            pltpu.SemaphoreType.DMA((peers,)),
            pltpu.SemaphoreType.DMA((peers,)),
            pltpu.SemaphoreType.REGULAR((max(n["lat"] - 1, 1),)),
        ],
        compiler_params=pltpu.CompilerParams(
            collective_id=0, has_side_effects=True, vmem_limit_bytes=59 * 1024 * 1024
        ),
    )(lat_taps, lon_taps, control, ensemble, precision, vertical)
    return hessian, curvature.reshape(())


def solution(mesh):
    axes = tuple(mesh.axis_names)
    sizes = tuple(mesh.shape[a] for a in axes)
    in_specs = (
        P("mem", "lat", "lon", None),
        P("mem", "lat", "lon", None),
        P("lat", "lon", None),
        P(),
        P(),
        P(),
    )
    out_specs = (P("mem", "lat", "lon", None), P())
    return jax.shard_map(
        functools.partial(per_device, axes, sizes),
        mesh=mesh, in_specs=in_specs, out_specs=out_specs, check_vma=False,
    )
```

```python
import functools
import itertools

import jax
import jax.numpy as jnp
from jax import lax
from jax.experimental import pallas as pl
from jax.experimental.pallas import tpu as pltpu
from jax.sharding import PartitionSpec as P

F32 = jnp.float32
BF16 = jnp.bfloat16
HALF = 4


def iota(shape, dim):
    return lax.broadcasted_iota(jnp.int32, shape, dim)


def tap_products(lat_taps, lon_taps, down, across, reverse):
    taps = lat_taps.shape[0]
    first = jnp.zeros(down.shape, F32)
    second = jnp.zeros(down.shape, F32)
    for tap in range(taps):
        at = taps - 1 - tap if reverse else tap
        first = jnp.where(down == tap, lat_taps[at], first)
        second = jnp.where(across == tap, lon_taps[at], second)
    full = first * second
    high = full.astype(BF16)
    low = (full - high.astype(F32)).astype(BF16)
    return jnp.concatenate([high, low], axis=0)


def full_matrix(lat_taps, lon_taps, cols, reverse):
    shape = (HALF * cols, 3 * HALF * cols + 6 * HALF * HALF)
    out, src = iota(shape, 0), iota(shape, 1)
    main = 3 * HALF * cols
    side = 3 * HALF * HALF
    inside = src < main
    left = src < main + side
    packed = jnp.where(left, src - main, src - main - side)
    row = jnp.where(inside, src // cols, packed // HALF)
    col = jnp.where(
        inside, src % cols, packed % HALF + jnp.where(left, -HALF, cols)
    )
    return tap_products(lat_taps, lon_taps, row - out // cols, col - out % cols + HALF, reverse)


def inner_matrix(lat_taps, lon_taps, cols, reverse):
    span = cols - 4 * HALF
    shape = (HALF * span, 3 * HALF * cols)
    out, src = iota(shape, 0), iota(shape, 1)
    down = src // cols - out // span
    across = src % cols - (out % span + 2 * HALF) + HALF
    return tap_products(lat_taps, lon_taps, down, across, reverse)


def rim_matrix(lat_taps, lon_taps, side, reverse):
    tile = 2 * HALF
    main = 3 * HALF * 2 * tile
    shape = (HALF * tile, main + 3 * HALF * HALF)
    out, src = iota(shape, 0), iota(shape, 1)
    inside = src < main
    packed = src - main
    row = jnp.where(inside, src // (2 * tile), packed // HALF)
    col = jnp.where(inside, src % (2 * tile), packed % HALF + (2 * tile if side else -HALF))
    down = row - out // tile
    across = col - (out % tile + (tile if side else 0)) + HALF
    return tap_products(lat_taps, lon_taps, down, across, reverse)


def dot(a, b):
    return jnp.dot(a, b, preferred_element_type=F32)


def kernel(
    axes, sizes, entries, chunks, lat_taps, lon_taps, control, ensemble, precision, vertical, hess, curv,
    ext, ext2, ens, prec, wgt, inners, rims, halo, halo2, stage, stage2,
    mid, near, far, filt2, vert, vert2, vert2t, sums, parts, norms, taps1, taps2,
    local_sem, row_send, row_recv, corner_send, corner_recv, side_send, side_recv, inc_send, inc_recv, part_sem, norm_send, norm_recv, met,
):
    members, rows, cols, levels = control.shape
    groups = rows // HALF
    per = groups // chunks
    cells = HALF * cols
    width = 2 if members % 2 == 0 else 1
    me = {a: lax.axis_index(a) for a in axes}
    n = dict(zip(axes, sizes))

    def device(**at):
        return tuple(at.get(a, me[a]) for a in axes)

    def place(to):
        index = 0
        for size, at in zip(sizes, to):
            index = index * size + at
        return index

    lat, lon = me["lat"], me["lon"]
    left = lax.rem(lon + n["lon"] - 1, n["lon"])
    right = lax.rem(lon + 1, n["lon"])
    has_up = lat > 0
    has_down = lat < n["lat"] - 1
    steps = [s for s in itertools.product(*(range(size) for size in sizes)) if any(s)]

    def ahead(step):
        return tuple(lax.rem(me[a] + d, n[a]) if d else me[a] for a, d in zip(axes, step))

    deep = per * HALF
    first_rows = 2 * deep + HALF
    head, tail = pl.ds(0, first_rows), pl.ds(first_rows, rows - first_rows)
    front, back_rows = pl.ds(deep, deep), pl.ds(2 * deep, rows - 2 * deep)
    loads = [
        pltpu.make_async_copy(control.at[:, head], ext.at[:, pl.ds(HALF, first_rows)], local_sem.at[0]),
        pltpu.make_async_copy(vertical, vert, local_sem.at[1]),
        pltpu.make_async_copy(ensemble.at[:, front], ens.at[:, front], local_sem.at[2]),
        pltpu.make_async_copy(ensemble.at[:, back_rows], ens.at[:, back_rows], local_sem.at[3]),
        pltpu.make_async_copy(lat_taps, taps1, local_sem.at[4]),
        pltpu.make_async_copy(lon_taps, taps2, local_sem.at[5]),
        pltpu.make_async_copy(ensemble.at[:, pl.ds(0, deep)], ens.at[:, pl.ds(0, deep)], local_sem.at[6]),
        pltpu.make_async_copy(precision, prec, local_sem.at[7]),
        pltpu.make_async_copy(
            control.at[:, tail], ext.at[:, pl.ds(HALF + first_rows, rows - first_rows)], local_sem.at[8]
        ),
    ]
    for at in (4, 5, 1, 0, 2, 8, 3, 6, 7):
        loads[at].start()

    barrier = pltpu.get_barrier_semaphore()
    plane = [s for s in steps if not s[axes.index("lat")]]

    def signal(semaphore, to):
        pl.semaphore_signal(semaphore, inc=1, device_id=to, device_id_type=pl.DeviceIdType.MESH)

    for step in plane:
        signal(barrier, ahead(step))
    for has, row in ((has_up, lat - 1), (has_down, lat + 1)):
        @pl.when(has)
        def _():
            for col in (lon, left, right):
                signal(barrier, device(lat=row, lon=col))
    beside = jnp.where(has_up, 1, 0) + jnp.where(has_down, 1, 0)

    def hello(turn):
        for has, row in ((has_up, lat - 1), (has_down, lat + 1)):
            @pl.when(has)
            def _():
                signal(met.at[turn], device(lat=row))

    def hear(turn):
        pl.semaphore_wait(met.at[turn], beside)

    def remote(src, dst, send, recv, to):
        return pltpu.make_async_remote_copy(
            src_ref=src, dst_ref=dst, send_sem=send, recv_sem=recv,
            device_id=to, device_id_type=pl.DeviceIdType.MESH,
        )

    def row_copies(phase, up_src, down_src, dst):
        up = remote(
            up_src, dst.at[:, pl.ds(rows + HALF, HALF)],
            row_send.at[phase, 0], row_recv.at[phase, 0], device(lat=lat - 1),
        )
        down = remote(
            down_src, dst.at[:, pl.ds(0, HALF)],
            row_send.at[phase, 1], row_recv.at[phase, 1], device(lat=lat + 1),
        )
        return [up], [down]

    def corner_copies(phase, src, dst):
        up, down = [], []
        for side, to in ((0, left), (1, right)):
            there = dst.at[1 - side]
            mine = src.at[side]
            up.append(remote(
                mine.at[:, 0], there.at[:, groups + 1],
                corner_send.at[phase, 0], corner_recv.at[phase, 0], device(lat=lat - 1, lon=to),
            ))
            down.append(remote(
                mine.at[:, groups - 1], there.at[:, 0],
                corner_send.at[phase, 1], corner_recv.at[phase, 1], device(lat=lat + 1, lon=to),
            ))
        return up, down

    def corner_waits(phase, src, dst):
        up = remote(
            src.at[:, :, 0], dst.at[:, :, groups + 1],
            corner_send.at[phase, 0], corner_recv.at[phase, 0], device(lat=lat - 1, lon=left),
        )
        down = remote(
            src.at[:, :, groups - 1], dst.at[:, :, 0],
            corner_send.at[phase, 1], corner_recv.at[phase, 1], device(lat=lat + 1, lon=left),
        )
        return [up], [down]

    half = chunks // 2
    sets = [[1, 2], *[[k] for k in range(3, half + 1)], [0], [chunks - 1, chunks], list(range(half + 1, chunks - 1))]
    sets = [ks for ks in sets if ks]

    def piece(phase, k):
        if phase == 1:
            return k * per, per
        ks = sets[k]
        start = max((ks[0] - 1) * per + 1, 0)
        return start, min(ks[-1] * per + 1, groups) - start

    def side_sem(phase, k):
        return side_recv.at[phase * len(sets) + k]

    def side_copies(phase, src, dst, k):
        at, size = piece(phase, k)
        return [
            remote(
                src.at[side, :, pl.ds(at, size)], dst.at[1 - side, :, pl.ds(at + 1, size)],
                side_send.at[phase], side_sem(phase, k), device(lon=to),
            )
            for side, to in ((0, left), (1, right))
        ]

    def side_arrival(phase, src, dst, k):
        at, size = piece(phase, k)
        return remote(
            src.at[:, :, pl.ds(at, size)], dst.at[:, :, pl.ds(at + 1, size)],
            side_send.at[phase], side_sem(phase, k), device(lon=left),
        )

    def inc_sem(chunk, part):
        return chunk if part else chunks + (chunk == 0) + 2 * (chunk == chunks - 1)

    def inc_copies(chunk, part):
        at = pl.ds(chunk * per, per)
        field = (inners, rims)[part].at[me["mem"], at]
        return [
            remote(
                field, field, inc_send.at[part, step - 1], inc_recv.at[step - 1, inc_sem(chunk, part)],
                device(mem=lax.rem(me["mem"] + step, n["mem"])),
            )
            for step in range(1, n["mem"])
        ]

    def inc_arrivals(chunk, part):
        first, count = chunk, 1
        if part == 0 and 0 < chunk < chunks - 1:
            if "inner" in arrived:
                return []
            arrived.add("inner")
            first, count = 1, chunks - 2
        at = pl.ds(first * per, count * per)
        arrivals = []
        for step in range(1, n["mem"]):
            peer = lax.rem(me["mem"] + n["mem"] - step, n["mem"])
            field = (inners, rims)[part].at[peer, at]
            arrivals.append(remote(
                field, field, inc_send.at[part, step - 1], inc_recv.at[step - 1, inc_sem(chunk, part)], device(mem=peer)
            ))
        return arrivals

    arrived = set()

    def each(has, copies, act):
        @pl.when(has)
        def _():
            for copy in copies:
                getattr(copy, act)()

    @pl.when(jnp.logical_not(has_up))
    def _():
        for one, two in ((ext, halo), (ext2, halo2)):
            one[:, 0:HALF] = jnp.zeros((members, HALF, cols, levels), BF16)
            for side in range(2):
                two[side, :, 0] = jnp.zeros((members, HALF * HALF, levels), BF16)

    @pl.when(jnp.logical_not(has_down))
    def _():
        for one, two in ((ext, halo), (ext2, halo2)):
            one[:, rows + HALF : rows + 2 * HALF] = jnp.zeros((members, HALF, cols, levels), BF16)
            for side in range(2):
                two[side, :, groups + 1] = jnp.zeros((members, HALF * HALF, levels), BF16)

    vert2[...] = jnp.zeros_like(vert2)
    with jax.named_scope("taps"):
        loads[4].wait()
        loads[5].wait()
    with jax.named_scope("filt"):
        mid[...] = inner_matrix(taps1, taps2, cols, False)

    first = iota((2 * HALF, levels), 0) < HALF

    def edges(block):
        tile = 2 * HALF
        near = [block[cols * r : cols * r + tile] for r in range(HALF)]
        far = [block[cols * (r + 1) - tile : cols * (r + 1)] for r in range(HALF)]
        lefts = [jnp.where(first, near[r], pltpu.roll(near[r + 1], HALF, 0)) for r in range(0, HALF, 2)]
        rights = [jnp.where(first, pltpu.roll(far[r], HALF, 0), far[r + 1]) for r in range(0, HALF, 2)]
        return jnp.concatenate(lefts, axis=0).astype(BF16), jnp.concatenate(rights, axis=0).astype(BF16)

    def pack_group(go, carry):
        for m in range(members):
            block = ext[m, pl.ds(HALF * (go + 1), HALF)].reshape(cells, levels).astype(F32)
            stage[0, m, go], stage[1, m, go] = edges(block)
        return carry

    tile = 2 * HALF
    blank = jnp.zeros((levels, levels), F32)

    def diagonal(block):
        if width == 1:
            return block.astype(BF16)
        return jnp.concatenate(
            [jnp.concatenate([block, blank], axis=1), jnp.concatenate([blank, block], axis=1)], axis=0
        ).astype(BF16)

    sums[...] = jnp.zeros_like(sums)

    def tile_sum(x):
        return jnp.sum(x.reshape(-1, 8, levels), axis=0)

    def squares(go, total):
        for m in range(members):
            block = ext[m, pl.ds(HALF * (go + 1), HALF)].reshape(cells, levels).astype(F32)
            total = total + tile_sum(block * block)
        return total

    def halves(matrix, data):
        both = dot(matrix[...], data)
        size = both.shape[0] // 2
        return both[:size] + both[size:]

    def smooth_inner(source, matrix, go, pair):
        data = [source[m, pl.ds(HALF * go, 3 * HALF)].reshape(3 * cells, levels) for m in pair]
        return halves(matrix, jnp.concatenate(data, axis=1))

    def smooth_rim(source, sides, matrices, go, pair):
        ends = []
        for side, matrix in enumerate(matrices):
            data = [
                jnp.concatenate([
                    source[m, pl.ds(HALF * go, 3 * HALF), (cols - 2 * tile) * side : (cols - 2 * tile) * side + 2 * tile]
                    .reshape(3 * HALF * 2 * tile, levels),
                    sides[side, m, pl.ds(go, 3)].reshape(3 * HALF * HALF, levels),
                ], axis=0)
                for m in pair
            ]
            ends.append(halves(matrix, jnp.concatenate(data, axis=1)))
        return jnp.concatenate(ends, axis=0)

    pairs = [tuple(range(m, m + width)) for m in range(0, members, width)]

    def inner_rows(x):
        return jnp.concatenate([x[cols * r + tile : cols * (r + 1) - tile] for r in range(HALF)], axis=0)

    def rim_rows(x):
        lefts = [x[cols * r : cols * r + tile] for r in range(HALF)]
        rights = [x[cols * (r + 1) - tile : cols * (r + 1)] for r in range(HALF)]
        return jnp.concatenate(lefts + rights, axis=0)

    def merge_rows(inner, rim):
        span = cols - 2 * tile
        blocks = []
        for r in range(HALF):
            blocks += [
                rim[tile * r : tile * (r + 1)], inner[span * r : span * (r + 1)],
                rim[tile * (HALF + r) : tile * (HALF + r + 1)],
            ]
        return jnp.concatenate(blocks, axis=0)

    def spread_of(m, go):
        return ens[m, pl.ds(HALF * go, HALF)].reshape(cells, levels).astype(F32)

    def contribute(places, smoothed, pick, field):
        leveled = dot(jnp.concatenate(smoothed, axis=0), vert2[...])
        size = leveled.shape[0] // len(smoothed)
        at = 0
        for go in places:
            total = None
            for pair in pairs:
                level = leveled[at : at + size]
                at += size
                for j, m in enumerate(pair):
                    term = pick(spread_of(m, go)) * level[:, j * levels : (j + 1) * levels]
                    total = term if total is None else total + term
            field[me["mem"], go] = total.astype(BF16)

    def places_of(chunk):
        return [chunk * per + g for g in range(per)]

    def forward_inner(chunk):
        places = places_of(chunk)
        smoothed = [smooth_inner(ext, mid, go, pair).astype(BF16) for go in places for pair in pairs]
        contribute(places, smoothed, inner_rows, inners)

    def forward_rim(some):
        places = [go for chunk in some for go in places_of(chunk)]
        smoothed = [smooth_rim(ext, halo, (near, far), go, pair).astype(BF16) for go in places for pair in pairs]
        contribute(places, smoothed, rim_rows, rims)

    def weigh(chunk):
        for g in range(per):
            go = chunk * per + g
            inner, rim = inners[0, go].astype(F32), rims[0, go].astype(F32)
            for peer in range(1, n["mem"]):
                inner = inner + inners[peer, go].astype(F32)
                rim = rim + rims[peer, go].astype(F32)
            increment = merge_rows(inner, rim)
            weighted = prec[pl.ds(HALF * go, HALF)].reshape(cells, levels) * increment
            sums[...] += tile_sum(weighted * increment)
            wgt[go] = weighted

    def adjoint(chunk):
        places = [chunk * per + g for g in range(per)]
        rows_of = []
        for go in places:
            weighted = wgt[go]
            for pair in pairs:
                parts_of = []
                for m in pair:
                    parts_of.append((spread_of(m, go) * weighted).astype(BF16))
                rows_of.append(jnp.concatenate(parts_of, axis=1))
        result = dot(jnp.concatenate(rows_of, axis=0), vert2t[...])
        at = 0
        for go in places:
            for pair in pairs:
                for j, m in enumerate(pair):
                    block = result[at : at + cells, j * levels : (j + 1) * levels]
                    ext2[m, pl.ds(HALF * (go + 1), HALF)] = block.astype(BF16).reshape(HALF, cols, levels)
                    stage2[0, m, go], stage2[1, m, go] = edges(block)
                at += cells
        for copy in side_copies(1, stage2, halo2, chunk):
            copy.start()

    def smooth(source, sides, matrix, go, pair):
        data = [
            jnp.concatenate([
                source[m, pl.ds(HALF * go, 3 * HALF)].reshape(3 * cells, levels),
                sides[0, m, pl.ds(go, 3)].reshape(3 * HALF * HALF, levels),
                sides[1, m, pl.ds(go, 3)].reshape(3 * HALF * HALF, levels),
            ], axis=0)
            for m in pair
        ]
        return halves(matrix, jnp.concatenate(data, axis=1))

    def final(chunk):
        for go in places_of(chunk):
            for pair in pairs:
                back = smooth(ext2, halo2, filt2, go, pair)
                for j, m in enumerate(pair):
                    held = ext[m, pl.ds(HALF * (go + 1), HALF)].astype(F32)
                    block = back[:, j * levels : (j + 1) * levels].reshape(HALF, cols, levels)
                    hess[m, pl.ds(HALF * go, HALF)] = held + block

    def wait_sides(phase, src, dst, chunk):
        side_arrival(phase, src, dst, chunk).wait_recv()

    row2_up, row2_down = row_copies(
        1, ext2.at[:, pl.ds(HALF, HALF)], ext2.at[:, pl.ds(rows, HALF)], ext2
    )
    corner2_up, corner2_down = corner_copies(1, stage2, halo2)
    both2_up, both2_down = corner_waits(1, stage2, halo2)

    across = [s for s in steps if not s[axes.index("mem")]]
    mine = lat * n["lon"] + lon
    part_out = [remote(parts.at[mine], parts.at[mine], part_sem.at[0], part_sem.at[1], ahead(step)) for step in across]
    others = parts.at[pl.ds(0, max(len(across), 1))]
    part_all = remote(others, others, part_sem.at[0], part_sem.at[1], ahead(steps[0]))
    norm = norms.at[me["mem"]]
    norm_out, norm_in = [], []
    for step in range(1, n["mem"]):
        to = lax.rem(me["mem"] + step, n["mem"])
        norm_out.append(remote(norm, norm, norm_send.at[step - 1], norm_recv.at[step - 1], device(mem=to)))
        of = lax.rem(me["mem"] + n["mem"] - step, n["mem"])
        norm_in.append(remote(norms.at[of], norms.at[of], norm_send.at[step - 1], norm_recv.at[step - 1], device(mem=of)))

    seen = {0: set(), 1: set()}

    def need_sides(phase, chunk):
        wanted = (chunk - 1, chunk, chunk + 1)
        if phase == 0:
            wanted = [i for i, ks in enumerate(sets) if chunk in ks or chunk + 1 in ks]
        for k in wanted:
            if 0 <= k < max(chunks, len(sets)) and k not in seen[phase] and piece(phase, k)[1] > 0:
                if phase == 1 and k >= chunks:
                    continue
                seen[phase].add(k)
                wait_sides(phase, *((stage, halo) if phase == 0 else (stage2, halo2)), k)

    row_up, row_down = row_copies(
        0, ext.at[:, pl.ds(HALF, HALF)], ext.at[:, pl.ds(rows, HALF)], ext
    )
    corner_up, corner_down = corner_copies(0, stage, halo)
    both_up, both_down = corner_waits(0, stage, halo)

    def start_inc(chunk, part):
        for copy in inc_copies(chunk, part):
            copy.start()

    def do_inner(chunk):
        if chunk == 0:
            with jax.named_scope("rowwait"):
                each(has_up, row_down, "wait_recv")
        if chunk == chunks - 1:
            with jax.named_scope("rowwait"):
                each(has_down, row_up, "wait_recv")
        with jax.named_scope("inner"):
            forward_inner(chunk)

    def do_rim(*some):
        with jax.named_scope("rimwait"):
            for chunk in some:
                need_sides(0, chunk)
                if chunk == 0:
                    each(has_up, both_down, "wait_recv")
                if chunk == chunks - 1:
                    each(has_down, both_up, "wait_recv")
        with jax.named_scope("rim"):
            forward_rim(some)
            for chunk in some:
                start_inc(chunk, 1)

    adjointed = set()

    def do_adjoint(chunk):
        with jax.named_scope("incwait"):
            for part in range(2):
                for copy in inc_arrivals(chunk, part):
                    copy.wait_recv()
        with jax.named_scope("weigh"):
            weigh(chunk)
        adjointed.add(chunk)
        if len(adjointed) == chunks:
            with jax.named_scope("part"):
                for copy in norm_in:
                    copy.wait_recv()
                total = sums[...]
                for peer in range(n["mem"]):
                    total = total + norms[peer]
                parts[mine] = jnp.sum(total, axis=0, keepdims=True)
                for copy in part_out:
                    copy.start()
        with jax.named_scope("adj"):
            adjoint(chunk)
            if chunk == 0:
                each(has_up, row2_up + corner2_up, "start")
            if chunk == chunks - 1:
                each(has_down, row2_down + corner2_down, "start")

    def do_final(chunk):
        with jax.named_scope("bwait"):
            need_sides(1, chunk)
            if chunk == 0:
                each(has_up, row2_down + both2_down, "wait_recv")
            if chunk == chunks - 1:
                each(has_down, row2_up + both2_up, "wait_recv")
        with jax.named_scope("fin"):
            final(chunk)

    middle = list(range(1, chunks - 1))
    turns = n["lat"] - 1
    with jax.named_scope("load1"):
        loads[1].wait()
    for j in range(width):
        vert2[j * levels : (j + 1) * levels, j * levels : (j + 1) * levels] = vert[...]
    with jax.named_scope("load0"):
        loads[0].wait()
        loads[2].wait()
    do_inner(middle[0])
    with jax.named_scope("barrier"):
        pl.semaphore_wait(barrier, len(plane) + 3 * beside)
    start_inc(middle[0], 0)
    with jax.named_scope("load8"):
        loads[8].wait()
    with jax.named_scope("pack"):
        lax.fori_loop(0, groups, pack_group, 0, unroll=4)
    waves = list(range(len(sets)))

    def send_sides():
        if not waves:
            return
        k = waves.pop(0)
        if piece(0, k)[1] > 0:
            for copy in side_copies(0, stage, halo, k):
                copy.start()
        if sets[k] == [0]:
            each(has_up, corner_up, "start")
            each(has_down, corner_down, "start")

    send_sides()
    each(has_up, row_up, "start")
    each(has_down, row_down, "start")
    while waves:
        send_sides()
    met_turns = []

    def meet():
        turn = len(met_turns)
        if turn > turns:
            return
        met_turns.append(turn)
        with jax.named_scope("meet"):
            if turn > 0:
                hear(turn - 1)
            if turn < turns:
                hello(turn)

    meet()
    with jax.named_scope("load3"):
        loads[3].wait()
        loads[6].wait()
    for chunk in middle[1:]:
        do_inner(chunk)
        start_inc(chunk, 0)
        send_sides()
        if chunk == middle[half - 1]:
            meet()
    while waves:
        send_sides()
    with jax.named_scope("filt1"):
        vert2t[...] = diagonal(vert[...].astype(F32).T)
        near[...] = rim_matrix(taps1, taps2, 0, False)
        far[...] = rim_matrix(taps1, taps2, 1, False)
    with jax.named_scope("squares"):
        norms[me["mem"]] = lax.fori_loop(0, groups, squares, jnp.zeros((8, levels), F32), unroll=2)
        for copy in norm_out:
            copy.start()
    with jax.named_scope("load7"):
        loads[7].wait()
    last = chunks - 1
    lead = middle[: half - 1]
    rest = [c for c in middle if c not in lead and c != last - 1]
    order = [*lead, 0, last, *rest, last - 1]

    def do_end(chunk):
        do_inner(chunk)
        start_inc(chunk, 0)

    for chunk in lead:
        do_rim(chunk)
        if chunk == lead[-1]:
            meet()
    do_end(0)
    do_rim(0)
    do_end(last)
    do_rim(last)
    ahead_of = half - 1
    do_adjoint(order[0])
    if rest:
        do_rim(*rest)
    do_adjoint(order[1])
    do_rim(last - 1)
    do_adjoint(order[2])
    do_adjoint(order[3])
    do_adjoint(order[4])
    with jax.named_scope("filt2"):
        filt2[...] = full_matrix(taps1, taps2, cols, True)
    while len(met_turns) <= turns:
        meet()
    done = {c: max(order.index(d) for d in (c - 1, c, c + 1)) for c in middle}
    finals = sorted(middle, key=lambda c: (done[c], c))
    slots = ()
    for now in order[ahead_of + 2 :]:
        do_adjoint(now)
        if order.index(now) in slots:
            do_final(finals.pop(0))
    for chunk in finals:
        do_final(chunk)
        if chunk == 1:
            do_final(0)
    do_final(last)

    with jax.named_scope("redend"):
        if across:
            part_all.wait_recv()
        curv[0, 0] = jnp.sum(parts[...]) * (1.0 / entries)

    with jax.named_scope("finish"):
        if across:
            part_all.wait_send()
        for copy in norm_out:
            copy.wait_send()
        each(has_up, row_up + both_up + row2_up + both2_up, "wait_send")
        each(has_down, row_down + both_down + row2_down + both2_down, "wait_send")
        for phase, src, dst in ((0, stage, halo), (1, stage2, halo2)):
            remote(src, dst.at[:, :, pl.ds(1, groups)], side_send.at[phase], side_recv.at[0], device(lon=left)).wait_send()
        for part, field in ((0, inners), (1, rims)):
            for step in range(1, n["mem"]):
                to = lax.rem(me["mem"] + step, n["mem"])
                whole = field.at[me["mem"]]
                remote(
                    whole, whole, inc_send.at[part, step - 1], inc_recv.at[step - 1, 0], device(mem=to)
                ).wait_send()


def per_device(axes, sizes, control, ensemble, precision, lat_taps, lon_taps, vertical):
    members, rows, cols, levels = control.shape
    n = dict(zip(axes, sizes))
    groups = rows // HALF
    cells = HALF * cols
    pack = HALF * HALF
    entries = control.size
    for size in sizes:
        entries *= size
    chunks = next(c for c in (8, 4, groups) if groups % c == 0)
    width = 2 if members % 2 == 0 else 1
    rim = 4 * pack
    smem = pl.BlockSpec(memory_space=pltpu.SMEM)
    anyspace = pl.BlockSpec(memory_space=pltpu.HBM)
    peers = max(n["mem"] - 1, 1)
    hessian, curvature = pl.pallas_call(
        functools.partial(kernel, axes, sizes, entries, chunks),
        out_shape=(
            pltpu.VMEM(control.shape, F32),
            jax.ShapeDtypeStruct((1, 1), F32),
        ),
        in_specs=[anyspace, anyspace, anyspace, anyspace, anyspace, anyspace],
        out_specs=(pl.BlockSpec(memory_space=pltpu.VMEM), smem),
        scratch_shapes=[
            pltpu.VMEM((members, rows + 2 * HALF, cols, levels), BF16),
            pltpu.VMEM((members, rows + 2 * HALF, cols, levels), BF16),
            pltpu.VMEM(control.shape, BF16),
            pltpu.VMEM(precision.shape, F32),
            pltpu.VMEM((groups, cells, levels), F32),
            pltpu.VMEM((n["mem"], groups, cells - rim, levels), BF16),
            pltpu.VMEM((n["mem"], groups, rim, levels), BF16),
            pltpu.VMEM((2, members, groups + 2, pack, levels), BF16),
            pltpu.VMEM((2, members, groups + 2, pack, levels), BF16),
            pltpu.VMEM((2, members, groups, pack, levels), BF16),
            pltpu.VMEM((2, members, groups, pack, levels), BF16),
            pltpu.VMEM((2 * (cells - rim), 3 * cells), BF16),
            pltpu.VMEM((rim, 15 * pack), BF16),
            pltpu.VMEM((rim, 15 * pack), BF16),
            pltpu.VMEM((2 * cells, 3 * cells + 6 * pack), BF16),
            pltpu.VMEM((levels, levels), BF16),
            pltpu.VMEM((width * levels, width * levels), BF16),
            pltpu.VMEM((width * levels, width * levels), BF16),
            pltpu.VMEM((8, levels), F32),
            pltpu.VMEM((n["lat"] * n["lon"], 1, levels), F32),
            pltpu.VMEM((n["mem"], 8, levels), F32),
            pltpu.SMEM(lat_taps.shape, F32),
            pltpu.SMEM(lon_taps.shape, F32),
            pltpu.SemaphoreType.DMA((9,)),
            pltpu.SemaphoreType.DMA((2, 2)),
            pltpu.SemaphoreType.DMA((2, 2)),
            pltpu.SemaphoreType.DMA((2, 2)),
            pltpu.SemaphoreType.DMA((2, 2)),
            pltpu.SemaphoreType.DMA((2,)),
            pltpu.SemaphoreType.DMA((chunks // 2 + chunks + 2,)),
            pltpu.SemaphoreType.DMA((2, peers)),
            pltpu.SemaphoreType.DMA((peers, chunks + 3)),
            pltpu.SemaphoreType.DMA((2,)),
            pltpu.SemaphoreType.DMA((peers,)),
            pltpu.SemaphoreType.DMA((peers,)),
            pltpu.SemaphoreType.REGULAR((max(n["lat"] - 1, 1),)),
        ],
        compiler_params=pltpu.CompilerParams(
            collective_id=0, has_side_effects=True, vmem_limit_bytes=59 * 1024 * 1024
        ),
    )(lat_taps, lon_taps, control, ensemble, precision, vertical)
    return hessian, curvature.reshape(())


def solution(mesh):
    axes = tuple(mesh.axis_names)
    sizes = tuple(mesh.shape[a] for a in axes)
    in_specs = (
        P("mem", "lat", "lon", None),
        P("mem", "lat", "lon", None),
        P("lat", "lon", None),
        P(),
        P(),
        P(),
    )
    out_specs = (P("mem", "lat", "lon", None), P())
    return jax.shard_map(
        functools.partial(per_device, axes, sizes),
        mesh=mesh, in_specs=in_specs, out_specs=out_specs, check_vma=False,
    )
```
